768 devices in a mesh: comp: 4 (over x), tile: 24 (over y, z_lo), rep: 8 (over z_hi, core).
Axes of the slice: x: 4, y: 8, z: 12 (z_hi: 4, z_lo: 3; z = z_hi * 3 + z_lo), core: 2. Of those that a mesh axis runs over, the one named last changes fastest.
Arguments:
- retarded: bfloat16 [2, 384, 2, 192, 192], P(None, ('tile', 'rep')), may hold values from -0.3125 to 0.3125
- self_energy: bfloat16 [4, 384, 2, 192, 192], P('comp', ('tile', 'rep')), may hold values from -6 to 6
- energy_of: int32 [384], replicated, may hold values from 0 to 383, each once
Outputs:
- polar: float32 [4, 384, 2, 192, 192], P('comp', 'tile', None, 'rep')
The draws below stay inside these ranges and needn't reach their ends.
Inputs may be any that keep to these rules, and one draw needn't show every extreme that they name: `energy_of`: each of the 384 energy grid indices stands in exactly one slot.
All inputs are finite; a program needn't handle non-finite values.
Results may differ from the reference program's by a relative error of at most 0.0095.
Values may be sent and summed in bfloat16 or wider, within the bound.
No kernel may reach another device: no remote copies, remote signals or barrier semaphores. Data moves between devices by JAX's collectives and lax.ppermute only.
A program may use at most 32 MiB of HBM per device.

```python
import math
import jax
import jax.numpy as jnp
from jax import lax

NB = 192
NE = 384


def block_scale(stream_key, shape, cuts, smallest, largest):
    factor_of = 1.0
    for dim, blocks in cuts:
        heights = jax.random.uniform(jax.random.fold_in(jax.random.fold_in(stream_key, 6), dim), (blocks,), jnp.float32, smallest / len(cuts), largest / len(cuts))
        factor_of = factor_of * jnp.repeat(jnp.exp(heights), shape[dim] // blocks).reshape((-1,) + (1,) * (len(shape) - 1 - dim))
    return factor_of


def scatter_about(own_key, dims, spread, bound, shards=(), held_as=jnp.bfloat16):
    result = jax.random.normal(own_key, dims, jnp.float32) * spread
    if len(shards) > 0:
        result = block_scale(own_key, dims, shards, -0.22, 0.18) * result
    return jnp.clip(result, min=-bound, max=bound).astype(held_as)


def setup_inputs(seed: int = 0) -> dict:
    key_list = jax.random.split(jax.random.key(seed), 4)
    retarded = scatter_about(key_list[0], (2, NE, 2, NB, NB), (2 * NB) ** -0.5, 0.3125, ((1, 192),))
    self_energy = scatter_about(key_list[1], (4, NE, 2, NB, NB), 1.0, 6.0, ((0, 4), (1, 192)))
    energy_of = jax.random.permutation(key_list[2], NE).astype(jnp.int32)
    return {"retarded": retarded, "self_energy": self_energy, "energy_of": energy_of}


def product(left_side, right_side):
    return jnp.dot(left_side, right_side, preferred_element_type=jnp.float32)

def triple(operands):
    green_matrix, sigma_matrix = operands
    green_re, green_im = (green_matrix[0], green_matrix[1])
    sigma_re, sigma_im = (sigma_matrix[0], sigma_matrix[1])
    left_re = (product(green_re, sigma_re) - product(green_im, sigma_im)).astype(jnp.bfloat16)
    left_im = (product(green_re, sigma_im) + product(green_im, sigma_re)).astype(jnp.bfloat16)
    out_re = product(left_re, green_re.T) + product(left_im, green_im.T)
    out_im = product(left_im, green_re.T) - product(left_re, green_im.T)
    return jnp.stack([out_re, out_im]).astype(jnp.bfloat16)

def reference(retarded, self_energy, energy_of):
    slot_count = energy_of.shape[0]
    freq_count = 2 * slot_count
    forward = []
    backward = []
    for component in range(4):
        green_all = lax.map(triple, (retarded[component // 2], self_energy[component]))
        if component % 2 == 1:
            green_all = jnp.swapaxes(green_all, 2, 3)
        ordered = jnp.zeros_like(green_all).at[energy_of].set(green_all)
        signal = ordered[:, 0].astype(jnp.float32) + 1j * ordered[:, 1].astype(jnp.float32)
        spectrum = jnp.fft.fft(signal, n=freq_count, axis=0)
        forward.append(spectrum)
        backward.append(jnp.concatenate([spectrum[:1], jnp.flip(spectrum[1:], axis=0)], axis=0))
    results = []
    for component in range(4):
        joint = forward[component] * backward[component ^ 1]
        joint_re = jnp.real(joint).astype(jnp.bfloat16).astype(jnp.float32)
        joint_im = jnp.imag(joint).astype(jnp.bfloat16).astype(jnp.float32)
        lagged = jnp.fft.ifft(joint_re + 1j * joint_im, axis=0)[:slot_count]
        polar_value = -1j * lagged / math.sqrt(slot_count)
        results.append(jnp.stack([jnp.real(polar_value), jnp.imag(polar_value)], axis=1))
    return jnp.stack(results).astype(jnp.float32)
```

```python
import functools
import math

import jax
import jax.numpy as jnp
import numpy as np
from jax import lax
from jax.experimental import pallas as pl
from jax.experimental.pallas import tpu as pltpu
from jax.sharding import Mesh, PartitionSpec as P

LANES = 128
INTERPRET = False


def twiddles(count):
    steps = (2 * np.arange(count)[:, None] + 1) * np.arange(count)[None, :] % (4 * count)
    angles = steps * (math.pi / (2 * count))
    return np.cos(angles), np.sin(angles)


def batched(left_side, right_side, pattern):
    return jnp.einsum(pattern, left_side, right_side, preferred_element_type=jnp.float32)


def dot(left_side, right_side):
    return jnp.dot(left_side, right_side, preferred_element_type=jnp.float32)


def forward_sums(signal, energy, table):
    count = energy.shape[1]
    grid_index = lax.broadcasted_iota(jnp.int32, (count, count), 0)
    pick = (grid_index == energy).astype(jnp.float32).astype(jnp.bfloat16)
    ordered = dot(pick, signal).astype(jnp.bfloat16)
    return dot(table, ordered)


def forward_kernel(signal_ref, energy_ref, table_ref, out_ref):
    out_ref[...] = forward_sums(signal_ref[...], energy_ref[...], table_ref[...])


def times(left, right):
    left_re, left_im = left[:, :LANES], left[:, LANES:]
    right_re, right_im = right[:, :LANES], right[:, LANES:]
    return left_re * right_re - left_im * right_im, left_re * right_im + left_im * right_re


def correlate_kernel(sign_ref, signal_ref, energy_ref, table_ref, own_ref, back_cos_ref, back_sin_ref, out_ref, *, scale):
    count = energy_ref.shape[1]
    other = forward_sums(signal_ref[...], energy_ref[...], table_ref[...])
    own_cos, own_sin = own_ref[:count, :], own_ref[count:, :]
    other_cos, other_sin = other[:count], other[count:]
    sign = sign_ref[0]
    even_parts = [a + b for a, b in zip(times(own_cos, other_cos), times(own_sin, other_sin))]
    odd_parts = [(a - b) * sign for a, b in zip(times(own_sin, other_cos), times(own_cos, other_sin))]
    even = dot(back_cos_ref[...], jnp.concatenate(even_parts, axis=1).astype(jnp.bfloat16))
    odd = dot(back_sin_ref[...], jnp.concatenate(odd_parts, axis=1).astype(jnp.bfloat16))
    for member, total in enumerate((even + odd, even - odd)):
        out_ref[member, :, :LANES] = (total[:, LANES:] * scale).astype(out_ref.dtype)
        out_ref[member, :, LANES:] = (total[:, :LANES] * -scale).astype(out_ref.dtype)


def body(retarded, self_energy, energy_of, *, sizes):
    tile_count, rep_count = sizes
    member = lax.axis_index("mem")
    momentum = lax.axis_index("pair")
    green_matrix = lax.dynamic_index_in_dim(retarded, momentum, 0, keepdims=False)
    sigma_matrix = self_energy[0]
    green_re, green_im = (green_matrix[:, 0], green_matrix[:, 1])
    sigma_re, sigma_im = (sigma_matrix[:, 0], sigma_matrix[:, 1])
    left_re = (
        batched(green_re, sigma_re, "eik,ekj->eij") - batched(green_im, sigma_im, "eik,ekj->eij")
    ).astype(jnp.bfloat16)
    left_im = (
        batched(green_re, sigma_im, "eik,ekj->eij") + batched(green_im, sigma_re, "eik,ekj->eij")
    ).astype(jnp.bfloat16)
    out_re = batched(left_re, green_re, "eik,ejk->eij") + batched(left_im, green_im, "eik,ejk->eij")
    out_im = batched(left_im, green_re, "eik,ejk->eij") - batched(left_re, green_im, "eik,ejk->eij")
    stacked = jnp.stack([out_re, out_im]).astype(jnp.bfloat16)
    stacked = jnp.where(member == 1, jnp.swapaxes(stacked, 2, 3), stacked)

    energy_dev, order = stacked.shape[1], stacked.shape[2]
    slot_count = energy_of.shape[0]
    half = order // 2
    blocks = stacked.reshape(2, energy_dev, rep_count, tile_count, 2, half)
    blocks = blocks.transpose(3, 2, 1, 4, 0, 5).reshape(tile_count * rep_count, energy_dev, 2 * order)
    gathered = lax.all_to_all(blocks, ("tile", "rep"), split_axis=0, concat_axis=0, tiled=True)
    halves = gathered.reshape(slot_count, 2, 2, half)
    away = lax.dynamic_index_in_dim(halves, 1 - member, 1, keepdims=False)
    partner = lax.ppermute(away.reshape(slot_count, order), "mem", [(0, 1), (1, 0)]).reshape(slot_count, 2, half)
    here = lax.dynamic_index_in_dim(halves, member, 1, keepdims=False)

    def spread(part):
        return jnp.pad(part, ((0, 0), (0, 0), (0, LANES - half))).reshape(slot_count, 2 * LANES)

    cos_part, sin_part = twiddles(slot_count)
    table = jnp.asarray(np.concatenate([cos_part, sin_part]), jnp.bfloat16)
    back_cos, back_sin = jnp.asarray(cos_part.T, jnp.bfloat16), jnp.asarray(sin_part.T, jnp.bfloat16)
    energy = energy_of.reshape(1, slot_count)
    own = pl.pallas_call(
        forward_kernel,
        out_shape=jax.ShapeDtypeStruct((2 * slot_count, 2 * LANES), jnp.float32),
        interpret=INTERPRET,
        name="own_sums",
    )(spread(here), energy, table)
    sign = (1 - 2 * member).astype(jnp.float32).reshape(1)
    vmem = pl.BlockSpec(memory_space=pltpu.VMEM)
    polar = pl.pallas_call(
        functools.partial(correlate_kernel, scale=2.0 / (2 * slot_count * math.sqrt(slot_count))),
        out_shape=jax.ShapeDtypeStruct((2, slot_count, 2 * LANES), jnp.bfloat16),
        in_specs=[pl.BlockSpec(memory_space=pltpu.SMEM)] + [vmem] * 6,
        interpret=INTERPRET,
        name="correlate",
    )(sign, spread(partner), energy, table, own, back_cos, back_sin)
    lag_count = slot_count // tile_count
    packed = polar.reshape(2, slot_count, 2, LANES)[..., :half].reshape(2 * tile_count, lag_count // 2, 2 * order)
    regrouped = lax.all_to_all(packed, ("mem", "tile"), split_axis=0, concat_axis=0, tiled=True)
    regrouped = regrouped.reshape(2, tile_count, lag_count, 2, half).transpose(2, 3, 1, 0, 4)
    return regrouped.reshape(1, lag_count, 2, tile_count, order).astype(jnp.float32)


def solution(mesh):
    comp, tile, rep = mesh.devices.shape
    split = Mesh(mesh.devices.reshape(2, comp // 2, tile, rep), ("pair", "mem", "tile", "rep"))
    placed = (
        P(None, ("tile", "rep"), None, None, None),
        P(("pair", "mem"), ("tile", "rep"), None, None, None),
        P(),
    )
    return jax.shard_map(
        functools.partial(body, sizes=(tile, rep)),
        mesh=split,
        in_specs=placed,
        out_specs=P(("pair", "mem"), "tile", None, "rep", None),
        check_vma=False,
    )
```

```python
import functools
import math

import jax
import jax.numpy as jnp
import numpy as np
from jax import lax
from jax.experimental import pallas as pl
from jax.experimental.pallas import tpu as pltpu
from jax.sharding import Mesh, PartitionSpec as P

LANES = 128
INTERPRET = False


def twiddles(count):
    steps = (2 * np.arange(count)[:, None] + 1) * np.arange(count)[None, :] % (4 * count)
    angles = steps * (math.pi / (2 * count))
    return np.cos(angles), np.sin(angles)


def dot(left_side, right_side):
    return jnp.dot(left_side, right_side, preferred_element_type=jnp.float32)


def dot_rows(left_side, right_side):
    return lax.dot_general(left_side, right_side, (((1,), (1,)), ((), ())), preferred_element_type=jnp.float32)


def one_hot(condition):
    return jnp.where(condition, 1.0, 0.0).astype(jnp.bfloat16)


def triple_kernel(place_ref, retarded_ref, self_energy_ref, out_ref, green_ref, sigma_ref, left_ref, right_ref, sems, *, sizes):
    tile_count, rep_count = sizes
    energies, _, order, _ = green_ref.shape
    half = order // 2
    copies = []
    for e in range(energies):
        pair = (
            pltpu.make_async_copy(retarded_ref.at[place_ref[0], e], green_ref.at[e], sems.at[e, 0]),
            pltpu.make_async_copy(self_energy_ref.at[0, e], sigma_ref.at[e], sems.at[e, 1]),
        )
        for copy in pair:
            copy.start()
        copies.append(pair)
    target = lax.broadcasted_iota(jnp.int32, (2 * order, 2 * order), 0)
    source = lax.broadcasted_iota(jnp.int32, (2 * order, 2 * order), 1)
    device, side = target >> 1, target & 1
    row = (device & (rep_count - 1)) * tile_count + (device >> (rep_count.bit_length() - 1))
    arrange = one_hot(source == side * order + row)
    sides = ([], [])
    for e in range(energies):
        for copy in copies[e]:
            copy.wait()
        green_re, green_im = green_ref[e, 0], green_ref[e, 1]
        sigma_re, sigma_im = sigma_ref[e, 0], sigma_ref[e, 1]
        cross_re = (dot(green_re, sigma_re) - dot(green_im, sigma_im)).astype(jnp.bfloat16)
        cross_im = (dot(green_re, sigma_im) + dot(green_im, sigma_re)).astype(jnp.bfloat16)

        def set_sides(left_re, left_im, right_re, right_im, conj, own):
            left_ref[0], left_ref[1] = left_re, left_im
            for side, start in enumerate((own * half, (1 - own) * half)):
                re, im = right_re[start : start + half], right_im[start : start + half]
                right_ref[side, 0, :half], right_ref[side, 0, half:] = re, -im if conj else im
                right_ref[side, 1, :half], right_ref[side, 1, half:] = im, re if conj else -re

        @pl.when(place_ref[1] == 0)
        def _():
            set_sides(cross_re, cross_im, green_re, green_im, True, 0)

        @pl.when(place_ref[1] == 1)
        def _():
            set_sides(green_re, green_im, cross_re, cross_im, False, 1)

        for side in range(2):
            sides[side].append(
                dot_rows(left_ref[0], right_ref[side, 0]) + dot_rows(left_ref[1], right_ref[side, 1])
            )
    stacked = jnp.concatenate([jnp.concatenate(s, axis=1) for s in sides], axis=0).astype(jnp.bfloat16)
    out_ref[...] = dot(arrange, stacked).astype(jnp.bfloat16)


def forward_sums(signal, energy, table, ordered_ref):
    energies, devices = energy.shape
    half = signal.shape[1] // (2 * energies)
    grid_index = lax.broadcasted_iota(jnp.int32, (energies * devices, devices), 0)
    picks = [one_hot(grid_index == energy[e : e + 1]) for e in range(energies)]
    ordered_ref[...] = jnp.zeros(ordered_ref.shape, ordered_ref.dtype)
    for part in range(2):
        total = None
        for e in range(energies):
            start = (2 * e + part) * half
            term = dot(picks[e], signal[:, start : start + half])
            total = term if total is None else total + term
        ordered_ref[:, part * LANES : part * LANES + half] = total.astype(jnp.bfloat16)
    return dot(table, ordered_ref[...])


def forward_kernel(signal_ref, energy_ref, table_ref, out_ref, ordered_ref):
    out_ref[...] = forward_sums(signal_ref[...], energy_ref[...], table_ref[...], ordered_ref)


def times(left, right):
    left_re, left_im = left[:, :LANES], left[:, LANES:]
    right_re, right_im = right[:, :LANES], right[:, LANES:]
    return left_re * right_re - left_im * right_im, left_re * right_im + left_im * right_re


def correlate_kernel(
    sign_ref, signal_ref, energy_ref, table_ref, own_ref, back_cos_ref, back_sin_ref, out_ref, ordered_ref, *, scale
):
    count = ordered_ref.shape[0]
    half = signal_ref.shape[1] // 4
    other = forward_sums(signal_ref[...], energy_ref[...], table_ref[...], ordered_ref)
    own_cos, own_sin = own_ref[:count, :], own_ref[count:, :]
    other_cos, other_sin = other[:count], other[count:]
    sign = sign_ref[0]
    even_parts = [a + b for a, b in zip(times(own_cos, other_cos), times(own_sin, other_sin))]
    odd_parts = [(a - b) * sign for a, b in zip(times(own_sin, other_cos), times(own_cos, other_sin))]
    even = dot(back_cos_ref[...], jnp.concatenate(even_parts, axis=1).astype(jnp.bfloat16))
    odd = dot(back_sin_ref[...], jnp.concatenate(odd_parts, axis=1).astype(jnp.bfloat16))
    rows = count // 2
    for member, total in enumerate((even + odd, even - odd)):
        re = total[:, LANES : LANES + half] * scale
        im = total[:, :half] * -scale
        out_ref[member] = jnp.concatenate([re[:rows], im[:rows], re[rows:], im[rows:]], axis=1).astype(out_ref.dtype)


def on_chip(array):
    return pltpu.with_memory_space_constraint(array, pltpu.VMEM) if not INTERPRET else array


def on_chip_out(shape, dtype):
    return pltpu.VMEM(shape, dtype) if not INTERPRET else jax.ShapeDtypeStruct(shape, dtype)


def body(retarded, self_energy, energy_of, *, sizes):
    tile_count, rep_count = sizes
    device_count = tile_count * rep_count
    member = lax.axis_index("mem")
    momentum = lax.axis_index("pair")
    energies, order = retarded.shape[1], retarded.shape[3]
    half = order // 2
    slot_count = energy_of.shape[0]
    in_vmem = pl.BlockSpec(memory_space=pltpu.VMEM)
    in_smem = pl.BlockSpec(memory_space=pltpu.SMEM)
    in_place = pl.BlockSpec(memory_space=pl.ANY)
    blocks = pl.pallas_call(
        functools.partial(triple_kernel, sizes=sizes),
        out_shape=on_chip_out((2 * device_count, 2 * energies * half), jnp.bfloat16),
        in_specs=[in_smem, in_place, in_place],
        out_specs=in_vmem,
        scratch_shapes=[
            pltpu.VMEM((energies, 2, order, order), jnp.bfloat16),
            pltpu.VMEM((energies, 2, order, order), jnp.bfloat16),
            pltpu.VMEM((2, order, order), jnp.bfloat16),
            pltpu.VMEM((2, 2, order, order), jnp.bfloat16),
            pltpu.SemaphoreType.DMA((energies, 2)),
        ],
        interpret=INTERPRET,
        name="triple",
    )(jnp.stack([momentum, member]), retarded, self_energy)
    blocks = blocks.reshape(device_count, 2, 2 * energies * half)
    gathered = lax.all_to_all(blocks, ("tile", "rep"), split_axis=0, concat_axis=0, tiled=True)
    partner = lax.ppermute(gathered[:, 1], "mem", [(0, 1), (1, 0)])

    cos_part, sin_part = twiddles(slot_count)
    table = on_chip(jnp.asarray(np.concatenate([cos_part, sin_part]), jnp.bfloat16))
    lag_count = slot_count // tile_count
    lags = np.arange(slot_count).reshape(tile_count, 2, lag_count // 2).transpose(1, 0, 2).reshape(-1)
    back_cos = on_chip(jnp.asarray(cos_part.T[lags], jnp.bfloat16))
    back_sin = on_chip(jnp.asarray(sin_part.T[lags], jnp.bfloat16))
    energy = on_chip(energy_of.reshape(device_count, energies).T)
    ordered = pltpu.VMEM((slot_count, 2 * LANES), jnp.bfloat16)
    own = pl.pallas_call(
        forward_kernel,
        out_shape=on_chip_out((2 * slot_count, 2 * LANES), jnp.float32),
        in_specs=[in_vmem] * 3,
        out_specs=in_vmem,
        scratch_shapes=[ordered],
        interpret=INTERPRET,
        name="own_sums",
    )(on_chip(gathered[:, 0]), energy, table)
    sign = (1 - 2 * member).astype(jnp.float32).reshape(1)
    polar = pl.pallas_call(
        functools.partial(correlate_kernel, scale=2.0 / (2 * slot_count * math.sqrt(slot_count))),
        out_shape=on_chip_out((2, slot_count // 2, 4 * half), jnp.bfloat16),
        in_specs=[in_smem] + [in_vmem] * 6,
        out_specs=in_vmem,
        scratch_shapes=[ordered],
        interpret=INTERPRET,
        name="correlate",
    )(sign, on_chip(partner), energy, table, own, back_cos, back_sin)
    packed = polar.reshape(2 * tile_count, lag_count // 2, 4 * half)
    regrouped = lax.all_to_all(packed, ("mem", "tile"), split_axis=0, concat_axis=0, tiled=True)
    regrouped = regrouped.reshape(2, tile_count, lag_count // 2, 2, 2, half).transpose(3, 2, 4, 1, 0, 5)
    return regrouped.reshape(1, lag_count, 2, tile_count, order).astype(jnp.float32)


def solution(mesh):
    comp, tile, rep = mesh.devices.shape
    split = Mesh(mesh.devices.reshape(2, comp // 2, tile, rep), ("pair", "mem", "tile", "rep"))
    placed = (
        P(None, ("tile", "rep"), None, None, None),
        P(("pair", "mem"), ("tile", "rep"), None, None, None),
        P(),
    )
    return jax.shard_map(
        functools.partial(body, sizes=(tile, rep)),
        mesh=split,
        in_specs=placed,
        out_specs=P(("pair", "mem"), "tile", None, "rep", None),
        check_vma=False,
    )
```

```python
import functools
import math

import jax
import jax.numpy as jnp
import numpy as np
from jax import lax
from jax.experimental import pallas as pl
from jax.experimental.pallas import tpu as pltpu
from jax.sharding import Mesh, PartitionSpec as P

LANES = 128
INTERPRET = False


def twiddles(count):
    steps = (2 * np.arange(count)[:, None] + 1) * np.arange(count)[None, :] % (4 * count)
    angles = steps * (math.pi / (2 * count))
    return np.cos(angles), np.sin(angles)


def dot(left_side, right_side):
    return jnp.dot(left_side, right_side, preferred_element_type=jnp.float32)


def dot_rows(left_side, right_side):
    return lax.dot_general(left_side, right_side, (((1,), (1,)), ((), ())), preferred_element_type=jnp.float32)


def one_hot(condition):
    return jnp.where(condition, 1.0, 0.0).astype(jnp.bfloat16)


def triple_kernel(retarded_ref, self_energy_ref, own_ref, away_ref, green_ref, sigma_ref, left_ref, right_ref, sems, *, sizes):
    tile_count, hop_count = sizes
    energies, _, order, _ = green_ref.shape
    half = order // 2
    momentum, member, core = lax.axis_index("pair"), lax.axis_index("mem"), lax.axis_index("core")
    copies = []
    for e in range(energies):
        pair = (
            pltpu.make_async_copy(retarded_ref.at[momentum, e], green_ref.at[e], sems.at[e, 0]),
            pltpu.make_async_copy(self_energy_ref.at[0, e], sigma_ref.at[e], sems.at[e, 1]),
        )
        for copy in pair:
            copy.start()
        copies.append(pair)
    target = lax.broadcasted_iota(jnp.int32, (order, order), 0)
    source = lax.broadcasted_iota(jnp.int32, (order, order), 1)
    away = jnp.where(target >= half, 1, 0)
    device = target - away * half
    to_core = core + away - 2 * core * away
    row = (2 * (device & (hop_count - 1)) + to_core) * tile_count + (device >> (hop_count.bit_length() - 1))
    pick = one_hot(source == row)
    sums = []
    for e in range(energies):
        for copy in copies[e]:
            copy.wait()
        green_re, green_im = green_ref[e, 0], green_ref[e, 1]
        sigma_re, sigma_im = sigma_ref[e, 0], sigma_ref[e, 1]
        cross_re = (dot(green_re, sigma_re) - dot(green_im, sigma_im)).astype(jnp.bfloat16)
        cross_im = (dot(green_re, sigma_im) + dot(green_im, sigma_re)).astype(jnp.bfloat16)

        def set_sides(left_re, left_im, right_re, right_im, conj):
            left_ref[0], left_ref[1] = left_re, left_im
            for side in range(2):
                re, im = right_re[side * half : (side + 1) * half], right_im[side * half : (side + 1) * half]
                right_ref[side, 0, :half], right_ref[side, 0, half:] = re, -im if conj else im
                right_ref[side, 1, :half], right_ref[side, 1, half:] = im, re if conj else -re

        @pl.when(member == 0)
        def _():
            set_sides(cross_re, cross_im, green_re, green_im, True)

        @pl.when(member == 1)
        def _():
            set_sides(green_re, green_im, cross_re, cross_im, False)

        left = [dot(pick, left_ref[part]).astype(jnp.bfloat16) for part in range(2)]
        sums.append(
            [dot_rows(left[0], right_ref[side, 0]) + dot_rows(left[1], right_ref[side, 1]) for side in range(2)]
        )
    for start, out_ref in ((0, own_ref), (half, away_ref)):
        for side in range(2):
            out_ref[side * half : (side + 1) * half] = jnp.concatenate(
                [sums[e][side][start : start + half] for e in range(energies)], axis=1
            ).astype(jnp.bfloat16)


def times(left, right):
    left_re, left_im = left[:, :LANES], left[:, LANES:]
    right_re, right_im = right[:, :LANES], right[:, LANES:]
    return left_re * right_re - left_im * right_im, left_re * right_im + left_im * right_re


def correlate_kernel(signal_ref, energy_ref, table_ref, back_cos_ref, back_sin_ref, out_ref, ordered_ref, *, scale):
    energies, devices = energy_ref.shape
    count = energies * devices
    half = signal_ref.shape[1] // (2 * energies)
    grid_index = lax.broadcasted_iota(jnp.int32, (count, devices), 0)
    picks = [one_hot(grid_index == energy_ref[e : e + 1]) for e in range(energies)]
    ordered_ref[...] = jnp.zeros(ordered_ref.shape, ordered_ref.dtype)
    for component in range(2):
        signal = signal_ref[component * devices : (component + 1) * devices]
        for part in range(2):
            total = None
            for e in range(energies):
                start = (2 * e + part) * half
                term = dot(picks[e], signal[:, start : start + half])
                total = term if total is None else total + term
            lane = (2 * component + part) * LANES
            ordered_ref[:, lane : lane + half] = total.astype(jnp.bfloat16)
    one_cos, one_sin = (dot(table_ref[r * count : (r + 1) * count], ordered_ref[:, : 2 * LANES]) for r in range(2))
    two_cos, two_sin = (dot(table_ref[r * count : (r + 1) * count], ordered_ref[:, 2 * LANES :]) for r in range(2))
    even_parts = [a + b for a, b in zip(times(one_cos, two_cos), times(one_sin, two_sin))]
    odd_parts = [a - b for a, b in zip(times(one_sin, two_cos), times(one_cos, two_sin))]
    even = dot(back_cos_ref[...], jnp.concatenate(even_parts, axis=1).astype(jnp.bfloat16))
    odd = dot(back_sin_ref[...], jnp.concatenate(odd_parts, axis=1).astype(jnp.bfloat16))
    rows = count // 2
    for component, total in enumerate((even + odd, even - odd)):
        re = total[:, LANES : LANES + half] * scale
        im = total[:, :half] * -scale
        out_ref[component] = jnp.concatenate([re[:rows], im[:rows], re[rows:], im[rows:]], axis=1).astype(out_ref.dtype)


def on_chip(array):
    return pltpu.with_memory_space_constraint(array, pltpu.VMEM) if not INTERPRET else array


def on_chip_out(shape, dtype):
    return pltpu.VMEM(shape, dtype) if not INTERPRET else jax.ShapeDtypeStruct(shape, dtype)


def body(retarded, self_energy, energy_of, *, sizes):
    tile_count, hop_count = sizes
    energies, order = retarded.shape[1], retarded.shape[3]
    half = order // 2
    slot_count = energy_of.shape[0]
    in_vmem = pl.BlockSpec(memory_space=pltpu.VMEM)
    in_place = pl.BlockSpec(memory_space=pl.ANY)
    block = on_chip_out((order, 2 * energies * half), jnp.bfloat16)
    own, away = pl.pallas_call(
        functools.partial(triple_kernel, sizes=sizes),
        out_shape=(block, block),
        in_specs=[in_place, in_place],
        out_specs=(in_vmem, in_vmem),
        scratch_shapes=[
            pltpu.VMEM((energies, 2, order, order), jnp.bfloat16),
            pltpu.VMEM((energies, 2, order, order), jnp.bfloat16),
            pltpu.VMEM((2, order, order), jnp.bfloat16),
            pltpu.VMEM((2, 2, order, order), jnp.bfloat16),
            pltpu.SemaphoreType.DMA((energies, 2)),
        ],
        interpret=INTERPRET,
        name="triple",
    )(retarded, self_energy)
    sibling = lax.ppermute(away, "core", [(0, 1), (1, 0)])
    by_core = energy_of.reshape(slot_count // (2 * energies), 2, energies)
    by_core = jnp.where(lax.axis_index("core") == 0, by_core, by_core[:, ::-1])
    energy = by_core.reshape(slot_count // energies, energies).T
    blocks, energy = lax.optimization_barrier((jnp.stack([own, sibling], axis=1), energy))
    gathered = lax.all_to_all(blocks, ("mem", "tile", "zh"), split_axis=0, concat_axis=0, tiled=True)

    cos_part, sin_part = twiddles(slot_count)
    table = on_chip(jnp.asarray(np.concatenate([cos_part, sin_part]), jnp.bfloat16))
    lag_count = slot_count // tile_count
    lags = np.arange(slot_count).reshape(tile_count, 2, lag_count // 2).transpose(1, 0, 2).reshape(-1)
    back_cos = on_chip(jnp.asarray(cos_part.T[lags], jnp.bfloat16))
    back_sin = on_chip(jnp.asarray(sin_part.T[lags], jnp.bfloat16))
    polar = pl.pallas_call(
        functools.partial(correlate_kernel, scale=2.0 / (2 * slot_count * math.sqrt(slot_count))),
        out_shape=on_chip_out((2, slot_count // 2, 4 * half), jnp.bfloat16),
        in_specs=[in_vmem] * 5,
        out_specs=in_vmem,
        scratch_shapes=[pltpu.VMEM((slot_count, 4 * LANES), jnp.bfloat16)],
        interpret=INTERPRET,
        name="correlate",
    )(on_chip(gathered.reshape(2 * order, 2 * energies * half)), on_chip(energy), table, back_cos, back_sin)
    packed = polar.reshape(2 * tile_count, lag_count // 2, 4 * half)
    regrouped = lax.all_to_all(packed, ("mem", "tile"), split_axis=0, concat_axis=0, tiled=True)
    regrouped = regrouped.reshape(2, tile_count, lag_count // 2, 2, 2, half).transpose(3, 2, 4, 1, 0, 5)
    return regrouped.reshape(1, lag_count, 2, tile_count, order).astype(jnp.float32)


def solution(mesh):
    comp, tile, rep = mesh.devices.shape
    split = Mesh(mesh.devices.reshape(2, comp // 2, tile, rep // 2, 2), ("pair", "mem", "tile", "zh", "core"))
    energy_axes = ("tile", "zh", "core")
    placed = (
        P(None, energy_axes, None, None, None),
        P(("pair", "mem"), energy_axes, None, None, None),
        P(),
    )
    return jax.shard_map(
        functools.partial(body, sizes=(tile, rep // 2)),
        mesh=split,
        in_specs=placed,
        out_specs=P(("pair", "mem"), "tile", None, ("zh", "core"), None),
        check_vma=False,
    )
```

```python
import functools
import math

import jax
import jax.numpy as jnp
import numpy as np
from jax import lax
from jax.experimental import pallas as pl
from jax.experimental.pallas import tpu as pltpu
from jax.sharding import Mesh, PartitionSpec as P

LANES = 128
INTERPRET = False


def twiddles(count):
    steps = (2 * np.arange(count)[:, None] + 1) * np.arange(count)[None, :] % (4 * count)
    angles = steps * (math.pi / (2 * count))
    return np.cos(angles), np.sin(angles)


def dot(left_side, right_side):
    return jnp.dot(left_side, right_side, preferred_element_type=jnp.float32)


def dot_rows(left_side, right_side):
    return lax.dot_general(left_side, right_side, (((1,), (1,)), ((), ())), preferred_element_type=jnp.float32)


def one_hot(condition):
    return jnp.where(condition, 1.0, 0.0).astype(jnp.bfloat16)


def triple_kernel(
    retarded_ref, self_energy_ref, energy_ref, table_ref, own_ref, away_ref, energy_out_ref, table_out_ref,
    green_ref, sigma_ref, left_ref, right_ref, sems, *, sizes
):
    tile_count, hop_count = sizes
    energies, _, order, _ = green_ref.shape
    half = order // 2
    momentum, member, core = lax.axis_index("pair"), lax.axis_index("mem"), lax.axis_index("core")
    copies = []
    for e in range(energies):
        pair = (
            pltpu.make_async_copy(retarded_ref.at[momentum, e], green_ref.at[e], sems.at[e, 0]),
            pltpu.make_async_copy(self_energy_ref.at[0, e], sigma_ref.at[e], sems.at[e, 1]),
        )
        for copy in pair:
            copy.start()
        copies.append(pair)
    copies.append(
        (
            pltpu.make_async_copy(energy_ref, energy_out_ref, sems.at[energies, 0]),
            pltpu.make_async_copy(table_ref, table_out_ref, sems.at[energies, 1]),
        )
    )
    for copy in copies[energies]:
        copy.start()
    target = lax.broadcasted_iota(jnp.int32, (order, order), 0)
    source = lax.broadcasted_iota(jnp.int32, (order, order), 1)
    away = jnp.where(target >= half, 1, 0)
    device = target - away * half
    to_core = core + away - 2 * core * away
    row = (2 * (device & (hop_count - 1)) + to_core) * tile_count + (device >> (hop_count.bit_length() - 1))
    pick = one_hot(source == row)
    sums = []
    for e in range(energies):
        for copy in copies[e]:
            copy.wait()
        green_re, green_im = green_ref[e, 0], green_ref[e, 1]
        sigma_re, sigma_im = sigma_ref[e, 0], sigma_ref[e, 1]
        cross_re = (dot(green_re, sigma_re) - dot(green_im, sigma_im)).astype(jnp.bfloat16)
        cross_im = (dot(green_re, sigma_im) + dot(green_im, sigma_re)).astype(jnp.bfloat16)

        def set_sides(left_re, left_im, right_re, right_im, conj):
            left_ref[0], left_ref[1] = left_re, left_im
            for side in range(2):
                re, im = right_re[side * half : (side + 1) * half], right_im[side * half : (side + 1) * half]
                right_ref[side, 0, :half], right_ref[side, 0, half:] = re, -im if conj else im
                right_ref[side, 1, :half], right_ref[side, 1, half:] = im, re if conj else -re

        @pl.when(member == 0)
        def _():
            set_sides(cross_re, cross_im, green_re, green_im, True)

        @pl.when(member == 1)
        def _():
            set_sides(green_re, green_im, cross_re, cross_im, False)

        left = [dot(pick, left_ref[part]).astype(jnp.bfloat16) for part in range(2)]
        sums.append(
            [dot_rows(left[0], right_ref[side, 0]) + dot_rows(left[1], right_ref[side, 1]) for side in range(2)]
        )
    for start, out_ref in ((0, own_ref), (half, away_ref)):
        for side in range(2):
            out_ref[side * half : (side + 1) * half] = jnp.concatenate(
                [sums[e][side][start : start + half] for e in range(energies)], axis=1
            ).astype(jnp.bfloat16)
    for copy in copies[energies]:
        copy.wait()


def pick_kernel(energy_ref, out_ref):
    energies, count, devices = out_ref.shape
    core = lax.axis_index("core")
    slots = jnp.concatenate([energy_ref[r : r + 1] for r in range(energy_ref.shape[0])], axis=1)
    digit = lax.broadcasted_iota(jnp.int32, (16, count), 0)
    digits = jnp.where(digit == 0, slots >> 1, slots & 1).astype(jnp.float32).astype(jnp.bfloat16)
    slot = lax.broadcasted_iota(jnp.int32, (count, devices), 0)
    device = lax.broadcasted_iota(jnp.int32, (count, devices), 1)
    side = device & 1
    first = ((device >> 1) * 2 + side + core - 2 * side * core) * energies
    for e in range(energies):
        taken = dot(digits, one_hot(slot == first + e))
        out_ref[e] = one_hot(slot == (2.0 * taken[:1] + taken[1:2]).astype(jnp.int32))


def times(left, right):
    left_re, left_im = left[:, :LANES], left[:, LANES:]
    right_re, right_im = right[:, :LANES], right[:, LANES:]
    return left_re * right_re - left_im * right_im, left_re * right_im + left_im * right_re


def correlate_kernel(signal_ref, pick_ref, table_ref, out_ref, *, scale):
    energies, count, devices = pick_ref.shape
    half = signal_ref.shape[1] // (2 * energies)
    gap = jnp.zeros((devices, LANES - half), jnp.bfloat16)
    sums = []
    for component in range(2):
        signal = signal_ref[component * devices : (component + 1) * devices]
        ordered = None
        for e in range(energies):
            re, im = (signal[:, (2 * e + part) * half : (2 * e + part + 1) * half] for part in range(2))
            term = dot(pick_ref[e], jnp.concatenate([re, gap, im, gap], axis=1))
            ordered = term if ordered is None else ordered + term
        ordered = ordered.astype(jnp.bfloat16)
        sums.append([dot(table_ref[r * count : (r + 1) * count], ordered) for r in range(2)])
    (one_cos, one_sin), (two_cos, two_sin) = sums
    even_parts = [a + b for a, b in zip(times(one_cos, two_cos), times(one_sin, two_sin))]
    odd_parts = [a - b for a, b in zip(times(one_sin, two_cos), times(one_cos, two_sin))]
    even = dot(table_ref[2 * count : 3 * count], jnp.concatenate(even_parts, axis=1).astype(jnp.bfloat16))
    odd = dot(table_ref[3 * count :], jnp.concatenate(odd_parts, axis=1).astype(jnp.bfloat16))
    rows = count // 2
    for component, total in enumerate((even + odd, even - odd)):
        re = total[:, LANES : LANES + half] * scale
        im = total[:, :half] * -scale
        out_ref[component] = jnp.concatenate([re[:rows], im[:rows], re[rows:], im[rows:]], axis=1).astype(out_ref.dtype)


def place_kernel(gathered_ref, out_ref, placed_ref, sems):
    _, lags, _, tiles, order = out_ref.shape
    half, low = order // 2, lags // 2
    rows = low * tiles
    target = lax.broadcasted_iota(jnp.int32, (rows, rows), 0)
    source = lax.broadcasted_iota(jnp.int32, (rows, rows), 1)
    pick = one_hot((source & (low - 1)) * tiles + (source >> (low.bit_length() - 1)) == target)
    copies = []
    for high in range(2):
        for part in range(2):
            lane = (2 * high + part) * half
            both = [gathered_ref[side * rows : (side + 1) * rows, lane : lane + half] for side in range(2)]
            moved = dot(pick, jnp.concatenate(both, axis=1))
            for lag in range(low):
                placed_ref[high, part, lag] = moved[lag * tiles : (lag + 1) * tiles]
            copies.append(
                pltpu.make_async_copy(
                    placed_ref.at[high, part], out_ref.at[0, pl.ds(high * low, low), part], sems.at[high, part]
                )
            )
            copies[-1].start()
    for copy in copies:
        copy.wait()


def on_chip(array):
    return pltpu.with_memory_space_constraint(array, pltpu.VMEM) if not INTERPRET else array


def on_chip_out(shape, dtype):
    return pltpu.VMEM(shape, dtype) if not INTERPRET else jax.ShapeDtypeStruct(shape, dtype)


def body(retarded, self_energy, energy_of, *, sizes):
    tile_count, hop_count = sizes
    energies, order = retarded.shape[1], retarded.shape[3]
    half = order // 2
    slot_count = energy_of.shape[0]
    in_vmem = pl.BlockSpec(memory_space=pltpu.VMEM)
    in_place = pl.BlockSpec(memory_space=pl.ANY)
    cos_part, sin_part = twiddles(slot_count)
    lag_count = slot_count // tile_count
    lags = np.arange(slot_count).reshape(tile_count, 2, lag_count // 2).transpose(1, 0, 2).reshape(-1)
    table = jnp.asarray(np.concatenate([cos_part, sin_part, cos_part.T[lags], sin_part.T[lags]]), jnp.bfloat16)
    lanes = math.gcd(slot_count, LANES)
    slot_energy = energy_of.reshape(slot_count // lanes, lanes)
    block = on_chip_out((order, 2 * energies * half), jnp.bfloat16)
    own, away, slot_energy, table = pl.pallas_call(
        functools.partial(triple_kernel, sizes=sizes),
        out_shape=(block, block, on_chip_out(slot_energy.shape, jnp.int32), on_chip_out(table.shape, jnp.bfloat16)),
        in_specs=[in_place] * 4,
        out_specs=(in_vmem,) * 4,
        scratch_shapes=[
            pltpu.VMEM((energies, 2, order, order), jnp.bfloat16),
            pltpu.VMEM((energies, 2, order, order), jnp.bfloat16),
            pltpu.VMEM((2, order, order), jnp.bfloat16),
            pltpu.VMEM((2, 2, order, order), jnp.bfloat16),
            pltpu.SemaphoreType.DMA((energies + 1, 2)),
        ],
        interpret=INTERPRET,
        name="triple",
    )(retarded, self_energy, slot_energy, table)
    sibling = lax.ppermute(away, "core", [(0, 1), (1, 0)])
    picks = pl.pallas_call(
        pick_kernel,
        out_shape=on_chip_out((energies, slot_count, slot_count // energies), jnp.bfloat16),
        in_specs=[in_vmem],
        out_specs=in_vmem,
        interpret=INTERPRET,
        name="picks",
    )(on_chip(slot_energy))
    blocks, picks = lax.optimization_barrier((jnp.stack([own, sibling], axis=1), picks))
    gathered = lax.all_to_all(blocks, ("mem", "tile", "zh"), split_axis=0, concat_axis=0, tiled=True)
    polar = pl.pallas_call(
        functools.partial(correlate_kernel, scale=2.0 / (2 * slot_count * math.sqrt(slot_count))),
        out_shape=on_chip_out((2, slot_count // 2, 4 * half), jnp.bfloat16),
        in_specs=[in_vmem] * 3,
        out_specs=in_vmem,
        interpret=INTERPRET,
        name="correlate",
    )(on_chip(gathered.reshape(2 * order, 2 * energies * half)), on_chip(picks), on_chip(table))
    packed = polar.reshape(2 * tile_count, lag_count // 2, 4 * half)
    regrouped = lax.all_to_all(packed, ("mem", "tile"), split_axis=0, concat_axis=0, tiled=True)
    return pl.pallas_call(
        place_kernel,
        out_shape=jax.ShapeDtypeStruct((1, lag_count, 2, tile_count, order), jnp.float32),
        in_specs=[in_vmem],
        out_specs=in_place,
        scratch_shapes=[
            pltpu.VMEM((2, 2, lag_count // 2, tile_count, order), jnp.float32),
            pltpu.SemaphoreType.DMA((2, 2)),
        ],
        interpret=INTERPRET,
        name="place",
    )(on_chip(regrouped.reshape(tile_count * lag_count, 4 * half)))


def solution(mesh):
    comp, tile, rep = mesh.devices.shape
    split = Mesh(mesh.devices.reshape(2, comp // 2, tile, rep // 2, 2), ("pair", "mem", "tile", "zh", "core"))
    energy_axes = ("tile", "zh", "core")
    placed = (
        P(None, energy_axes, None, None, None),
        P(("pair", "mem"), energy_axes, None, None, None),
        P(),
    )
    return jax.shard_map(
        functools.partial(body, sizes=(tile, rep // 2)),
        mesh=split,
        in_specs=placed,
        out_specs=P(("pair", "mem"), "tile", None, ("zh", "core"), None),
        check_vma=False,
    )
```

```python
import functools
import math

import jax
import jax.numpy as jnp
import numpy as np
from jax import lax
from jax.experimental import pallas as pl
from jax.experimental.pallas import tpu as pltpu
from jax.sharding import Mesh, PartitionSpec as P

LANES = 128
INTERPRET = False


def twiddles(count):
    steps = (2 * np.arange(count)[:, None] + 1) * np.arange(count)[None, :] % (4 * count)
    angles = steps * (math.pi / (2 * count))
    return np.cos(angles), np.sin(angles)


def dot(left_side, right_side):
    return jnp.dot(left_side, right_side, preferred_element_type=jnp.float32)


def dot_rows(left_side, right_side):
    return lax.dot_general(left_side, right_side, (((1,), (1,)), ((), ())), preferred_element_type=jnp.float32)


def one_hot(condition):
    return jnp.where(condition, 1.0, 0.0).astype(jnp.bfloat16)


def triple_kernel(
    retarded_ref, self_energy_ref, energy_ref, table_ref, own_ref, away_ref, energy_out_ref, table_out_ref,
    green_ref, sigma_ref, sems, *, sizes
):
    tile_count, hop_count = sizes
    energies, _, order, _ = green_ref.shape
    half = order // 2
    momentum, member, core = lax.axis_index("pair"), lax.axis_index("mem"), lax.axis_index("core")
    copies = []
    for e in range(energies):
        pair = (
            pltpu.make_async_copy(retarded_ref.at[momentum, e], green_ref.at[e], sems.at[e, 0]),
            pltpu.make_async_copy(self_energy_ref.at[0, e], sigma_ref.at[e], sems.at[e, 1]),
        )
        for copy in pair:
            copy.start()
        copies.append(pair)
    copies.append(
        (
            pltpu.make_async_copy(energy_ref, energy_out_ref, sems.at[energies, 0]),
            pltpu.make_async_copy(table_ref, table_out_ref, sems.at[energies, 1]),
        )
    )
    for copy in copies[energies]:
        copy.start()
    conj = jnp.where(member == 0, 1.0, -1.0)
    parts = []
    for e in range(energies):
        for copy in copies[e]:
            copy.wait()
        green = green_ref[e].reshape(2 * order, order)
        by_re, by_im = dot(green, sigma_ref[e, 0]), dot(green, sigma_ref[e, 1])
        cross = jnp.concatenate([by_re[:order] - by_im[order:], by_im[:order] + by_re[order:]], axis=0)
        cross = cross.astype(jnp.bfloat16)
        left, right = lax.select(member == 0, cross, green), lax.select(member == 0, green, cross)
        by_re, by_im = dot_rows(left, right[:order]), dot_rows(left, right[order:])
        parts.append((by_re[:order] + by_im[order:], (by_re[order:] - by_im[:order]) * conj))

    def rows_of(array, core):
        runs = [array[(2 * hop + core) * tile_count : (2 * hop + core + 1) * tile_count] for hop in range(hop_count)]
        return jnp.concatenate(runs, axis=0).astype(jnp.bfloat16)

    by_core = [[[rows_of(part, c) for part in pair] for pair in parts] for c in range(2)]
    for side in range(2):
        first, second = (
            jnp.concatenate([part[:, side * half : (side + 1) * half] for pair in rows for part in pair], axis=1)
            for rows in by_core
        )
        own_ref[side * half : (side + 1) * half] = lax.select(core == 0, first, second)
        away_ref[side * half : (side + 1) * half] = lax.select(core == 0, second, first)
    for copy in copies[energies]:
        copy.wait()


def pick_kernel(energy_ref, out_ref, *, sizes):
    tile_count, hop_count = sizes
    energies, count, devices = out_ref.shape
    core = lax.axis_index("core")
    slots = jnp.concatenate([energy_ref[r : r + 1] for r in range(energy_ref.shape[0])], axis=1)
    digit = lax.broadcasted_iota(jnp.int32, (16, count), 0)
    digits = jnp.where(digit == 0, slots >> 1, slots & 1).astype(jnp.float32).astype(jnp.bfloat16)
    slot = lax.broadcasted_iota(jnp.int32, (count, devices), 0)
    device = lax.broadcasted_iota(jnp.int32, (count, devices), 1)
    side = device & 1
    place = device >> 1
    hop = sum(jnp.where(place >= n * tile_count, 1, 0) for n in range(1, hop_count)) if hop_count > 1 else 0
    place = (place - hop * tile_count) * hop_count + hop
    first = (place * 2 + side + core - 2 * side * core) * energies
    for e in range(energies):
        taken = dot(digits, one_hot(slot == first + e))
        out_ref[e] = one_hot(slot == (2.0 * taken[:1] + taken[1:2]).astype(jnp.int32))


def times(left, right):
    left_re, left_im = left[:, :LANES], left[:, LANES:]
    right_re, right_im = right[:, :LANES], right[:, LANES:]
    return left_re * right_re - left_im * right_im, left_re * right_im + left_im * right_re


def correlate_kernel(signal_ref, pick_ref, table_ref, out_ref, ordered_ref, *, scale):
    energies, count, devices = pick_ref.shape
    half = signal_ref.shape[1] // (2 * energies)
    ordered_ref[...] = jnp.zeros(ordered_ref.shape, ordered_ref.dtype)
    sums = []
    for component in range(2):
        signal = signal_ref[component * devices : (component + 1) * devices]
        for part in range(2):
            starts = [(2 * e + part) * half for e in range(energies)]
            total = sum(dot(pick_ref[e], signal[:, start : start + half]) for e, start in enumerate(starts))
            ordered_ref[component, :, part * LANES : part * LANES + half] = total.astype(jnp.bfloat16)
        sums.append([dot(table_ref[r * count : (r + 1) * count], ordered_ref[component]) for r in range(2)])
    (one_cos, one_sin), (two_cos, two_sin) = sums
    even_parts = [a + b for a, b in zip(times(one_cos, two_cos), times(one_sin, two_sin))]
    odd_parts = [a - b for a, b in zip(times(one_sin, two_cos), times(one_cos, two_sin))]
    even = dot(table_ref[2 * count : 3 * count], jnp.concatenate(even_parts, axis=1).astype(jnp.bfloat16))
    odd = dot(table_ref[3 * count :], jnp.concatenate(odd_parts, axis=1).astype(jnp.bfloat16))
    rows = count // 2
    for component, total in enumerate((even + odd, even - odd)):
        re = total[:, LANES : LANES + half] * scale
        im = total[:, :half] * -scale
        out_ref[component] = jnp.concatenate([re[:rows], im[:rows], re[rows:], im[rows:]], axis=1).astype(out_ref.dtype)


def place_kernel(gathered_ref, out_ref, placed_ref, sems):
    _, lags, _, tiles, order = out_ref.shape
    half, low = order // 2, lags // 2
    rows = low * tiles
    target = lax.broadcasted_iota(jnp.int32, (rows, rows), 0)
    source = lax.broadcasted_iota(jnp.int32, (rows, rows), 1)
    pick = one_hot((source & (low - 1)) * tiles + (source >> (low.bit_length() - 1)) == target)
    copies = []
    for high in range(2):
        for part in range(2):
            lane = (2 * high + part) * half
            both = [gathered_ref[side * rows : (side + 1) * rows, lane : lane + half] for side in range(2)]
            moved = dot(pick, jnp.concatenate(both, axis=1))
            for lag in range(low):
                placed_ref[high, part, lag] = moved[lag * tiles : (lag + 1) * tiles]
            copies.append(
                pltpu.make_async_copy(
                    placed_ref.at[high, part], out_ref.at[0, pl.ds(high * low, low), part], sems.at[high, part]
                )
            )
            copies[-1].start()
    for copy in copies:
        copy.wait()


def on_chip(array):
    return pltpu.with_memory_space_constraint(array, pltpu.VMEM) if not INTERPRET else array


def on_chip_out(shape, dtype):
    return pltpu.VMEM(shape, dtype) if not INTERPRET else jax.ShapeDtypeStruct(shape, dtype)


def body(retarded, self_energy, energy_of, *, sizes):
    tile_count, hop_count = sizes
    energies, order = retarded.shape[1], retarded.shape[3]
    half = order // 2
    slot_count = energy_of.shape[0]
    in_vmem = pl.BlockSpec(memory_space=pltpu.VMEM)
    in_place = pl.BlockSpec(memory_space=pl.ANY)
    cos_part, sin_part = twiddles(slot_count)
    lag_count = slot_count // tile_count
    lags = np.arange(slot_count).reshape(tile_count, 2, lag_count // 2).transpose(1, 0, 2).reshape(-1)
    table = jnp.asarray(np.concatenate([cos_part, sin_part, cos_part.T[lags], sin_part.T[lags]]), jnp.bfloat16)
    lanes = math.gcd(slot_count, LANES)
    slot_energy = energy_of.reshape(slot_count // lanes, lanes)
    block = on_chip_out((order, 2 * energies * half), jnp.bfloat16)
    own, away, slot_energy, table = pl.pallas_call(
        functools.partial(triple_kernel, sizes=sizes),
        out_shape=(block, block, on_chip_out(slot_energy.shape, jnp.int32), on_chip_out(table.shape, jnp.bfloat16)),
        in_specs=[in_place] * 4,
        out_specs=(in_vmem,) * 4,
        scratch_shapes=[
            pltpu.VMEM((energies, 2, order, order), jnp.bfloat16),
            pltpu.VMEM((energies, 2, order, order), jnp.bfloat16),
            pltpu.SemaphoreType.DMA((energies + 1, 2)),
        ],
        interpret=INTERPRET,
        name="triple",
    )(retarded, self_energy, slot_energy, table)
    sibling = lax.ppermute(away, "core", [(0, 1), (1, 0)])
    picks = pl.pallas_call(
        functools.partial(pick_kernel, sizes=sizes),
        out_shape=on_chip_out((energies, slot_count, slot_count // energies), jnp.bfloat16),
        in_specs=[in_vmem],
        out_specs=in_vmem,
        interpret=INTERPRET,
        name="picks",
    )(on_chip(slot_energy))
    blocks, picks = lax.optimization_barrier((jnp.stack([own, sibling], axis=1), picks))
    gathered = lax.all_to_all(blocks, ("mem", "zh", "tile"), split_axis=0, concat_axis=0, tiled=True)
    polar = pl.pallas_call(
        functools.partial(correlate_kernel, scale=2.0 / (2 * slot_count * math.sqrt(slot_count))),
        out_shape=on_chip_out((2, slot_count // 2, 4 * half), jnp.bfloat16),
        in_specs=[in_vmem] * 3,
        out_specs=in_vmem,
        scratch_shapes=[pltpu.VMEM((2, slot_count, 2 * LANES), jnp.bfloat16)],
        interpret=INTERPRET,
        name="correlate",
    )(on_chip(gathered.reshape(2 * order, 2 * energies * half)), on_chip(picks), on_chip(table))
    packed = polar.reshape(2 * tile_count, lag_count // 2, 4 * half)
    regrouped = lax.all_to_all(packed, ("mem", "tile"), split_axis=0, concat_axis=0, tiled=True)
    return pl.pallas_call(
        place_kernel,
        out_shape=jax.ShapeDtypeStruct((1, lag_count, 2, tile_count, order), jnp.float32),
        in_specs=[in_vmem],
        out_specs=in_place,
        scratch_shapes=[
            pltpu.VMEM((2, 2, lag_count // 2, tile_count, order), jnp.float32),
            pltpu.SemaphoreType.DMA((2, 2)),
        ],
        interpret=INTERPRET,
        name="place",
    )(on_chip(regrouped.reshape(tile_count * lag_count, 4 * half)))


def solution(mesh):
    comp, tile, rep = mesh.devices.shape
    split = Mesh(mesh.devices.reshape(2, comp // 2, tile, rep // 2, 2), ("pair", "mem", "tile", "zh", "core"))
    energy_axes = ("tile", "zh", "core")
    placed = (
        P(None, energy_axes, None, None, None),
        P(("pair", "mem"), energy_axes, None, None, None),
        P(),
    )
    return jax.shard_map(
        functools.partial(body, sizes=(tile, rep // 2)),
        mesh=split,
        in_specs=placed,
        out_specs=P(("pair", "mem"), "tile", None, ("zh", "core"), None),
        check_vma=False,
    )
```

```python
import functools
import math

import jax
import jax.numpy as jnp
import numpy as np
from jax import lax
from jax.experimental import pallas as pl
from jax.experimental.pallas import tpu as pltpu
from jax.sharding import Mesh, PartitionSpec as P

LANES = 128
INTERPRET = False


def twiddles(count):
    steps = (2 * np.arange(count)[:, None] + 1) * np.arange(count)[None, :] % (4 * count)
    angles = steps * (math.pi / (2 * count))
    return np.cos(angles), np.sin(angles)


def dot(left_side, right_side):
    return jnp.dot(left_side, right_side, preferred_element_type=jnp.float32)


def dot_rows(left_side, right_side):
    return lax.dot_general(left_side, right_side, (((1,), (1,)), ((), ())), preferred_element_type=jnp.float32)


def one_hot(condition):
    return jnp.where(condition, 1.0, 0.0).astype(jnp.bfloat16)


def triple_kernel(
    retarded_ref, self_energy_ref, energy_ref, table_ref, own_ref, away_ref, energy_out_ref, table_out_ref,
    green_ref, sigma_ref, sems, *, sizes
):
    tile_count, hop_count = sizes
    energies, _, order, _ = green_ref.shape
    half = order // 2
    momentum, member, core = lax.axis_index("pair"), lax.axis_index("mem"), lax.axis_index("core")
    copies = []
    for e in range(energies):
        pair = (
            pltpu.make_async_copy(retarded_ref.at[momentum, e], green_ref.at[e], sems.at[e, 0]),
            pltpu.make_async_copy(self_energy_ref.at[0, e], sigma_ref.at[e], sems.at[e, 1]),
        )
        for copy in pair:
            copy.start()
        copies.append(pair)
    copies.append(
        (
            pltpu.make_async_copy(energy_ref, energy_out_ref, sems.at[energies, 0]),
            pltpu.make_async_copy(table_ref, table_out_ref, sems.at[energies, 1]),
        )
    )
    for copy in copies[energies]:
        copy.start()
    conj = jnp.where(member == 0, 1.0, -1.0)
    for e in range(energies):
        for copy in copies[e]:
            copy.wait()
    greens = [green_ref[e].reshape(2 * order, order) for e in range(energies)]
    first = [[dot(greens[e], sigma_ref[e, part]) for part in range(2)] for e in range(energies)]
    crosses = [
        jnp.concatenate([by_re[:order] - by_im[order:], by_im[:order] + by_re[order:]], axis=0).astype(jnp.bfloat16)
        for by_re, by_im in first
    ]
    parts = []
    for green, cross in zip(greens, crosses):
        left, right = lax.select(member == 0, cross, green), lax.select(member == 0, green, cross)
        by_re, by_im = dot_rows(left, right[:order]), dot_rows(left, right[order:])
        parts.append((by_re[:order] + by_im[order:], (by_re[order:] - by_im[:order]) * conj))

    def rows_of(array, core):
        runs = [array[(2 * hop + core) * tile_count : (2 * hop + core + 1) * tile_count] for hop in range(hop_count)]
        return jnp.concatenate(runs, axis=0).astype(jnp.bfloat16)

    by_core = [[[rows_of(part, c) for part in pair] for pair in parts] for c in range(2)]
    for side in range(2):
        first, second = (
            jnp.concatenate([part[:, side * half : (side + 1) * half] for pair in rows for part in pair], axis=1)
            for rows in by_core
        )
        own_ref[side * half : (side + 1) * half] = lax.select(core == 0, first, second)
        away_ref[side * half : (side + 1) * half] = lax.select(core == 0, second, first)
    for copy in copies[energies]:
        copy.wait()


def arrange_kernel(energy_ref, table_ref, out_ref, pick_ref, *, sizes):
    tile_count, hop_count = sizes
    count = pick_ref.shape[0]
    energies = count // (2 * tile_count * hop_count)
    devices = count // energies
    core = lax.axis_index("core")
    slots = jnp.concatenate([energy_ref[r : r + 1] for r in range(energy_ref.shape[0])], axis=1)
    digit = lax.broadcasted_iota(jnp.int32, (16, count), 0)
    digits = jnp.where(digit == 0, slots >> 1, slots & 1).astype(jnp.float32).astype(jnp.bfloat16)
    column = lax.broadcasted_iota(jnp.int32, (1, count), 1)
    energy = sum((jnp.where(column >= n * devices, 1, 0) for n in range(1, energies)), jnp.zeros_like(column))
    device = column - energy * devices
    side, place = device & 1, device >> 1
    hop = sum((jnp.where(place >= n * tile_count, 1, 0) for n in range(1, hop_count)), jnp.zeros_like(column))
    place = (place - hop * tile_count) * hop_count + hop
    wanted = (place * 2 + side + core - 2 * side * core) * energies + energy
    row = lax.broadcasted_iota(jnp.int32, (count, count), 0)
    taken = dot(digits, one_hot(row == wanted))
    pick_ref[...] = one_hot(row == (2.0 * taken[:1] + taken[1:2]).astype(jnp.int32))
    out_ref[...] = dot(table_ref[: 2 * count], pick_ref[...]).astype(jnp.bfloat16)


def times(left, right):
    return left[0] * right[0] - left[1] * right[1], left[0] * right[1] + left[1] * right[0]


def correlate_kernel(signal_ref, forward_ref, table_ref, out_ref, staged_ref):
    _, count, _ = staged_ref.shape
    devices = signal_ref.shape[0] // 2
    energies = count // devices
    half = signal_ref.shape[1] // (2 * energies)
    staged_ref[...] = jnp.zeros(staged_ref.shape, staged_ref.dtype)
    for component in range(2):
        signal = signal_ref[component * devices : (component + 1) * devices]
        for e in range(energies):
            for part in range(2):
                start = (2 * e + part) * half
                staged_ref[component, e * devices : (e + 1) * devices, part * LANES : part * LANES + half] = signal[
                    :, start : start + half
                ]
    spectra = []
    for component in range(2):
        cos_sum, sin_sum = (dot(forward_ref[r * count : (r + 1) * count], staged_ref[component]) for r in range(2))
        turned = (sin_sum[:, LANES:], -sin_sum[:, :LANES])
        plain = (cos_sum[:, :LANES], cos_sum[:, LANES:])
        spectra.append([[p + t for p, t in zip(plain, turned)], [p - t for p, t in zip(plain, turned)]])
    one, two = spectra
    ahead, behind = times(one[0], two[1]), times(one[1], two[0])
    even_parts = [ahead[0] + behind[0], ahead[1] + behind[1]]
    odd_parts = [behind[1] - ahead[1], ahead[0] - behind[0]]
    even = dot(table_ref[2 * count : 3 * count], jnp.concatenate(even_parts, axis=1).astype(jnp.bfloat16))
    odd = dot(table_ref[3 * count :], jnp.concatenate(odd_parts, axis=1).astype(jnp.bfloat16))
    rows = count // 2
    for component, total in enumerate((even + odd, even - odd)):
        total = total.astype(out_ref.dtype)
        im, re = total[:, LANES : LANES + half], total[:, :half]
        out_ref[component] = jnp.concatenate([im[:rows], re[:rows], im[rows:], re[rows:]], axis=1)


def place_kernel(gathered_ref, out_ref, placed_ref, sems, *, scale):
    _, lags, _, tiles, order = out_ref.shape
    half, low = order // 2, lags // 2
    rows = low * tiles
    target = lax.broadcasted_iota(jnp.int32, (rows, rows), 0)
    source = lax.broadcasted_iota(jnp.int32, (rows, rows), 1)
    pick = one_hot((source & (low - 1)) * tiles + (source >> (low.bit_length() - 1)) == target)
    copies = []
    for high in range(2):
        for part in range(2):
            lane = (2 * high + part) * half
            both = [gathered_ref[side * rows : (side + 1) * rows, lane : lane + half] for side in range(2)]
            moved = dot(pick, jnp.concatenate(both, axis=1)) * (-scale if part else scale)
            for lag in range(low):
                placed_ref[high, part, lag] = moved[lag * tiles : (lag + 1) * tiles]
            copies.append(
                pltpu.make_async_copy(
                    placed_ref.at[high, part], out_ref.at[0, pl.ds(high * low, low), part], sems.at[high, part]
                )
            )
            copies[-1].start()
    for copy in copies:
        copy.wait()


def on_chip(array):
    return pltpu.with_memory_space_constraint(array, pltpu.VMEM) if not INTERPRET else array


def on_chip_out(shape, dtype):
    return pltpu.VMEM(shape, dtype) if not INTERPRET else jax.ShapeDtypeStruct(shape, dtype)


def body(retarded, self_energy, energy_of, *, sizes):
    tile_count, hop_count = sizes
    energies, order = retarded.shape[1], retarded.shape[3]
    half = order // 2
    slot_count = energy_of.shape[0]
    in_vmem = pl.BlockSpec(memory_space=pltpu.VMEM)
    in_place = pl.BlockSpec(memory_space=pl.ANY)
    cos_part, sin_part = twiddles(slot_count)
    lag_count = slot_count // tile_count
    lags = np.arange(slot_count).reshape(tile_count, 2, lag_count // 2).transpose(1, 0, 2).reshape(-1)
    table = jnp.asarray(np.concatenate([cos_part, sin_part, cos_part.T[lags], sin_part.T[lags]]), jnp.bfloat16)
    lanes = math.gcd(slot_count, LANES)
    slot_energy = energy_of.reshape(slot_count // lanes, lanes)
    block = on_chip_out((order, 2 * energies * half), jnp.bfloat16)
    own, away, slot_energy, table = pl.pallas_call(
        functools.partial(triple_kernel, sizes=sizes),
        out_shape=(block, block, on_chip_out(slot_energy.shape, jnp.int32), on_chip_out(table.shape, jnp.bfloat16)),
        in_specs=[in_place] * 4,
        out_specs=(in_vmem,) * 4,
        scratch_shapes=[
            pltpu.VMEM((energies, 2, order, order), jnp.bfloat16),
            pltpu.VMEM((energies, 2, order, order), jnp.bfloat16),
            pltpu.SemaphoreType.DMA((energies + 1, 2)),
        ],
        interpret=INTERPRET,
        name="triple",
    )(retarded, self_energy, slot_energy, table)
    sibling = lax.ppermute(away, "core", [(0, 1), (1, 0)])
    forward = pl.pallas_call(
        functools.partial(arrange_kernel, sizes=sizes),
        out_shape=on_chip_out((2 * slot_count, slot_count), jnp.bfloat16),
        in_specs=[in_vmem] * 2,
        out_specs=in_vmem,
        scratch_shapes=[pltpu.VMEM((slot_count, slot_count), jnp.bfloat16)],
        interpret=INTERPRET,
        name="picks",
    )(on_chip(slot_energy), on_chip(table))
    blocks, forward = lax.optimization_barrier((jnp.stack([own, sibling], axis=1), forward))
    gathered = lax.all_to_all(blocks, ("mem", "zh", "tile"), split_axis=0, concat_axis=0, tiled=True)
    polar = pl.pallas_call(
        correlate_kernel,
        out_shape=on_chip_out((2, slot_count // 2, 4 * half), jnp.bfloat16),
        in_specs=[in_vmem] * 3,
        out_specs=in_vmem,
        scratch_shapes=[pltpu.VMEM((2, slot_count, 2 * LANES), jnp.bfloat16)],
        interpret=INTERPRET,
        name="correlate",
    )(on_chip(gathered.reshape(2 * order, 2 * energies * half)), on_chip(forward), on_chip(table))
    packed = polar.reshape(2 * tile_count, lag_count // 2, 4 * half)
    regrouped = lax.all_to_all(packed, ("mem", "tile"), split_axis=0, concat_axis=0, tiled=True)
    return pl.pallas_call(
        functools.partial(place_kernel, scale=1.0 / (2 * slot_count * math.sqrt(slot_count))),
        out_shape=jax.ShapeDtypeStruct((1, lag_count, 2, tile_count, order), jnp.float32),
        in_specs=[in_vmem],
        out_specs=in_place,
        scratch_shapes=[
            pltpu.VMEM((2, 2, lag_count // 2, tile_count, order), jnp.float32),
            pltpu.SemaphoreType.DMA((2, 2)),
        ],
        interpret=INTERPRET,
        name="place",
    )(on_chip(regrouped.reshape(tile_count * lag_count, 4 * half)))


def solution(mesh):
    comp, tile, rep = mesh.devices.shape
    split = Mesh(mesh.devices.reshape(2, comp // 2, tile, rep // 2, 2), ("pair", "mem", "tile", "zh", "core"))
    energy_axes = ("tile", "zh", "core")
    placed = (
        P(None, energy_axes, None, None, None),
        P(("pair", "mem"), energy_axes, None, None, None),
        P(),
    )
    return jax.shard_map(
        functools.partial(body, sizes=(tile, rep // 2)),
        mesh=split,
        in_specs=placed,
        out_specs=P(("pair", "mem"), "tile", None, ("zh", "core"), None),
        check_vma=False,
    )
```

```python
import functools
import math

import jax
import jax.numpy as jnp
import numpy as np
from jax import lax
from jax.experimental import pallas as pl
from jax.experimental.pallas import tpu as pltpu
from jax.sharding import Mesh, PartitionSpec as P

LANES = 128
INTERPRET = False
GRANT = 16 * 2**20
PLAIN = pltpu.CompilerParams(vmem_limit_bytes=GRANT)
SCHEDULE = pltpu.CompilerParams(vmem_limit_bytes=GRANT)


def twiddles(count):
    steps = (2 * np.arange(count)[:, None] + 1) * np.arange(count)[None, :] % (4 * count)
    angles = steps * (math.pi / (2 * count))
    return np.cos(angles), np.sin(angles)


def dot(left_side, right_side):
    return jnp.dot(left_side, right_side, preferred_element_type=jnp.float32)


def dot_rows(left_side, right_side):
    return lax.dot_general(left_side, right_side, (((1,), (1,)), ((), ())), preferred_element_type=jnp.float32)


def one_hot(condition):
    return jnp.where(condition, 1.0, 0.0).astype(jnp.bfloat16)


def write_blocks(out_ref, greens, crosses, to_core, sizes):
    tile_count, hop_count = sizes
    order = greens[0].shape[1]
    half = order // 2
    member = lax.axis_index("mem")
    conj = jnp.where(member == 0, 1.0, -1.0)

    def rows_of(array, core):
        starts = [part * order + (2 * hop + core) * tile_count for part in range(2) for hop in range(hop_count)]
        return jnp.concatenate([array[start : start + tile_count] for start in starts], axis=0)

    parts = []
    for green, cross in zip(greens, crosses):
        left, right = lax.select(member == 0, cross, green), lax.select(member == 0, green, cross)
        left = lax.select(to_core == 0, rows_of(left, 0), rows_of(left, 1))
        by_re, by_im = dot_rows(left, right[:order]), dot_rows(left, right[order:])
        parts.append((by_re[:half] + by_im[half:]).astype(jnp.bfloat16))
        parts.append(((by_re[half:] - by_im[:half]) * conj).astype(jnp.bfloat16))
    for side in range(2):
        out_ref[side * half : (side + 1) * half] = jnp.concatenate(
            [part[:, side * half : (side + 1) * half] for part in parts], axis=1
        )


def triple_kernel(
    retarded_ref, self_energy_ref, energy_ref, table_ref, away_ref, green_ref, cross_ref, energy_out_ref, table_out_ref,
    sigma_ref, sems, *, sizes
):
    energies, _, order, _ = green_ref.shape
    momentum, core = lax.axis_index("pair"), lax.axis_index("core")
    copies = []
    for e in range(energies):
        copies.append(pltpu.make_async_copy(retarded_ref.at[momentum, e], green_ref.at[e], sems.at[e, 0]))
        copies.append(pltpu.make_async_copy(self_energy_ref.at[0, e], sigma_ref.at[e], sems.at[e, 1]))
    later = (
        pltpu.make_async_copy(energy_ref, energy_out_ref, sems.at[energies, 0]),
        pltpu.make_async_copy(table_ref, table_out_ref, sems.at[energies, 1]),
    )
    for copy in (*copies, *later):
        copy.start()
    for copy in copies:
        copy.wait()
    greens = [green_ref[e].reshape(2 * order, order) for e in range(energies)]
    first = [[dot(greens[e], sigma_ref[e, part]) for part in range(2)] for e in range(energies)]
    crosses = [
        jnp.concatenate([by_re[:order] - by_im[order:], by_im[:order] + by_re[order:]], axis=0).astype(jnp.bfloat16)
        for by_re, by_im in first
    ]
    for e in range(energies):
        cross_ref[e] = crosses[e]
    write_blocks(away_ref, greens, crosses, 1 - core, sizes)
    for copy in later:
        copy.wait()


def arrange_kernel(green_ref, cross_ref, energy_ref, table_ref, own_ref, out_ref, pick_ref, *, sizes):
    tile_count, hop_count = sizes
    count = pick_ref.shape[0]
    energies = count // (2 * tile_count * hop_count)
    devices = count // energies
    core = lax.axis_index("core")
    both = range(green_ref.shape[0])
    greens = [green_ref[e].reshape(cross_ref.shape[1:]) for e in both]
    write_blocks(own_ref, greens, [cross_ref[e] for e in both], core, sizes)
    slots = jnp.concatenate([energy_ref[r : r + 1] for r in range(energy_ref.shape[0])], axis=1)
    digit = lax.broadcasted_iota(jnp.int32, (16, count), 0)
    digits = jnp.where(digit == 0, slots >> 1, slots & 1).astype(jnp.float32).astype(jnp.bfloat16)
    column = lax.broadcasted_iota(jnp.int32, (1, count), 1)
    energy = sum((jnp.where(column >= n * devices, 1, 0) for n in range(1, energies)), jnp.zeros_like(column))
    device = column - energy * devices
    side, place = device & 1, device >> 1
    hop = sum((jnp.where(place >= n * tile_count, 1, 0) for n in range(1, hop_count)), jnp.zeros_like(column))
    place = (place - hop * tile_count) * hop_count + hop
    wanted = (place * 2 + side + core - 2 * side * core) * energies + energy
    row = lax.broadcasted_iota(jnp.int32, (count, count), 0)
    taken = dot(digits, one_hot(row == wanted))
    pick_ref[...] = one_hot(row == (2.0 * taken[:1] + taken[1:2]).astype(jnp.int32))
    out_ref[...] = dot(table_ref[: 2 * count], pick_ref[...]).astype(jnp.bfloat16)


def times(left, right):
    return left[0] * right[0] - left[1] * right[1], left[0] * right[1] + left[1] * right[0]


def correlate_kernel(signal_ref, forward_ref, table_ref, out_ref, staged_ref):
    _, count, _ = staged_ref.shape
    devices = signal_ref.shape[0] // 2
    energies = count // devices
    half = signal_ref.shape[1] // (2 * energies)
    staged_ref[...] = jnp.zeros(staged_ref.shape, staged_ref.dtype)
    for component in range(2):
        signal = signal_ref[component * devices : (component + 1) * devices]
        for e in range(energies):
            for part in range(2):
                start = (2 * e + part) * half
                staged_ref[component, e * devices : (e + 1) * devices, part * LANES : part * LANES + half] = signal[
                    :, start : start + half
                ]
    spectra = []
    for component in range(2):
        cos_sum, sin_sum = (dot(forward_ref[r * count : (r + 1) * count], staged_ref[component]) for r in range(2))
        turned = (sin_sum[:, LANES:], -sin_sum[:, :LANES])
        plain = (cos_sum[:, :LANES], cos_sum[:, LANES:])
        spectra.append([[p + t for p, t in zip(plain, turned)], [p - t for p, t in zip(plain, turned)]])
    one, two = spectra
    ahead, behind = times(one[0], two[1]), times(one[1], two[0])
    even_parts = [ahead[0] + behind[0], ahead[1] + behind[1]]
    odd_parts = [behind[1] - ahead[1], ahead[0] - behind[0]]
    even = dot(table_ref[2 * count : 3 * count], jnp.concatenate(even_parts, axis=1).astype(jnp.bfloat16))
    odd = dot(table_ref[3 * count :], jnp.concatenate(odd_parts, axis=1).astype(jnp.bfloat16))
    rows = count // 2
    for component, total in enumerate((even + odd, even - odd)):
        total = total.astype(out_ref.dtype)
        im, re = total[:, LANES : LANES + half], total[:, :half]
        out_ref[component] = jnp.concatenate([im[:rows], re[:rows], im[rows:], re[rows:]], axis=1)


def place_kernel(gathered_ref, out_ref, placed_ref, sems, *, scale):
    _, lags, _, tiles, order = out_ref.shape
    half, low = order // 2, lags // 2
    rows = low * tiles
    target = lax.broadcasted_iota(jnp.int32, (rows, rows), 0)
    source = lax.broadcasted_iota(jnp.int32, (rows, rows), 1)
    pick = one_hot((source & (low - 1)) * tiles + (source >> (low.bit_length() - 1)) == target)
    copies = []
    for high in range(2):
        for part in range(2):
            lane = (2 * high + part) * half
            both = [gathered_ref[side * rows : (side + 1) * rows, lane : lane + half] for side in range(2)]
            moved = dot(pick, jnp.concatenate(both, axis=1)) * (-scale if part else scale)
            for lag in range(low):
                placed_ref[high, part, lag] = moved[lag * tiles : (lag + 1) * tiles]
            copies.append(
                pltpu.make_async_copy(
                    placed_ref.at[high, part], out_ref.at[0, pl.ds(high * low, low), part], sems.at[high, part]
                )
            )
            copies[-1].start()
    for copy in copies:
        copy.wait()


def on_chip(array):
    return pltpu.with_memory_space_constraint(array, pltpu.VMEM) if not INTERPRET else array


def off_chip(array):
    return pltpu.with_memory_space_constraint(array, pltpu.HBM) if not INTERPRET else array


def on_chip_out(shape, dtype):
    return pltpu.VMEM(shape, dtype) if not INTERPRET else jax.ShapeDtypeStruct(shape, dtype)


def body(retarded, self_energy, energy_of, *, sizes):
    tile_count, hop_count = sizes
    energies, order = retarded.shape[1], retarded.shape[3]
    half = order // 2
    slot_count = energy_of.shape[0]
    in_vmem = pl.BlockSpec(memory_space=pltpu.VMEM)
    in_place = pl.BlockSpec(memory_space=pl.ANY)
    cos_part, sin_part = twiddles(slot_count)
    lag_count = slot_count // tile_count
    lags = np.arange(slot_count).reshape(tile_count, 2, lag_count // 2).transpose(1, 0, 2).reshape(-1)
    table = jnp.asarray(np.concatenate([cos_part, sin_part, cos_part.T[lags], sin_part.T[lags]]), jnp.bfloat16)
    lanes = math.gcd(slot_count, LANES)
    slot_energy = energy_of.reshape(slot_count // lanes, lanes)
    block = on_chip_out((order, 2 * energies * half), jnp.bfloat16)
    greens = on_chip_out((energies, 2, order, order), jnp.bfloat16)
    crosses = on_chip_out((energies, 2 * order, order), jnp.bfloat16)
    away, green, cross, slot_energy, table = pl.pallas_call(
        functools.partial(triple_kernel, sizes=sizes),
        out_shape=(
            block,
            greens,
            crosses,
            on_chip_out(slot_energy.shape, jnp.int32),
            on_chip_out(table.shape, jnp.bfloat16),
        ),
        in_specs=[in_place] * 4,
        out_specs=(in_vmem,) * 5,
        scratch_shapes=[
            pltpu.VMEM((energies, 2, order, order), jnp.bfloat16),
            pltpu.SemaphoreType.DMA((energies + 1, 2)),
        ],
        compiler_params=SCHEDULE,
        interpret=INTERPRET,
        name="triple",
    )(*(off_chip(array) for array in (retarded, self_energy, slot_energy, table)))
    sibling = lax.ppermute(away, "core", [(0, 1), (1, 0)])
    own, forward = pl.pallas_call(
        functools.partial(arrange_kernel, sizes=sizes),
        out_shape=(block, on_chip_out((2 * slot_count, slot_count), jnp.bfloat16)),
        in_specs=[in_vmem] * 4,
        out_specs=(in_vmem,) * 2,
        scratch_shapes=[pltpu.VMEM((slot_count, slot_count), jnp.bfloat16)],
        compiler_params=SCHEDULE,
        interpret=INTERPRET,
        name="arrange",
    )(on_chip(green), on_chip(cross), on_chip(slot_energy), on_chip(table))
    blocks, forward = lax.optimization_barrier((jnp.stack([own, sibling], axis=1), forward))
    gathered = lax.all_to_all(blocks, ("mem", "zh", "tile"), split_axis=0, concat_axis=0, tiled=True)
    polar = pl.pallas_call(
        correlate_kernel,
        out_shape=on_chip_out((2, slot_count // 2, 4 * half), jnp.bfloat16),
        in_specs=[in_vmem] * 3,
        out_specs=in_vmem,
        scratch_shapes=[pltpu.VMEM((2, slot_count, 2 * LANES), jnp.bfloat16)],
        compiler_params=PLAIN,
        interpret=INTERPRET,
        name="correlate",
    )(on_chip(gathered.reshape(2 * order, 2 * energies * half)), on_chip(forward), on_chip(table))
    packed = polar.reshape(2 * tile_count, lag_count // 2, 4 * half)
    regrouped = lax.all_to_all(packed, ("mem", "tile"), split_axis=0, concat_axis=0, tiled=True)
    return pl.pallas_call(
        functools.partial(place_kernel, scale=1.0 / (2 * slot_count * math.sqrt(slot_count))),
        out_shape=jax.ShapeDtypeStruct((1, lag_count, 2, tile_count, order), jnp.float32),
        in_specs=[in_vmem],
        out_specs=in_place,
        scratch_shapes=[
            pltpu.VMEM((2, 2, lag_count // 2, tile_count, order), jnp.float32),
            pltpu.SemaphoreType.DMA((2, 2)),
        ],
        compiler_params=SCHEDULE,
        interpret=INTERPRET,
        name="place",
    )(on_chip(regrouped.reshape(tile_count * lag_count, 4 * half)))


def solution(mesh):
    comp, tile, rep = mesh.devices.shape
    split = Mesh(mesh.devices.reshape(2, comp // 2, tile, rep // 2, 2), ("pair", "mem", "tile", "zh", "core"))
    energy_axes = ("tile", "zh", "core")
    placed = (
        P(None, energy_axes, None, None, None),
        P(("pair", "mem"), energy_axes, None, None, None),
        P(),
    )
    return jax.shard_map(
        functools.partial(body, sizes=(tile, rep // 2)),
        mesh=split,
        in_specs=placed,
        out_specs=P(("pair", "mem"), "tile", None, ("zh", "core"), None),
        check_vma=False,
    )
```

```python
import functools
import math

import jax
import jax.numpy as jnp
import numpy as np
from jax import lax
from jax.experimental import pallas as pl
from jax.experimental.pallas import tpu as pltpu
from jax.sharding import Mesh, PartitionSpec as P

LANES = 128
INTERPRET = False
GRANT = 16 * 2**20
PLAIN = pltpu.CompilerParams(vmem_limit_bytes=GRANT)
SCHEDULE = pltpu.CompilerParams(vmem_limit_bytes=GRANT)


def twiddles(count):
    steps = (2 * np.arange(count)[:, None] + 1) * np.arange(count)[None, :] % (4 * count)
    angles = steps * (math.pi / (2 * count))
    return np.cos(angles), np.sin(angles)


def dot(left_side, right_side):
    return jnp.dot(left_side, right_side, preferred_element_type=jnp.float32)


def dot_rows(left_side, right_side):
    return lax.dot_general(left_side, right_side, (((1,), (1,)), ((), ())), preferred_element_type=jnp.float32)


def one_hot(condition):
    return jnp.where(condition, 1.0, 0.0).astype(jnp.bfloat16)


def write_blocks(out_ref, greens, crosses, to_core, sizes):
    tile_count, hop_count = sizes
    order = greens[0].shape[1]
    half = order // 2
    member = lax.axis_index("mem")
    conj = jnp.where(member == 0, 1.0, -1.0)

    def rows_of(array, core):
        starts = [part * order + (2 * hop + core) * tile_count for part in range(2) for hop in range(hop_count)]
        return jnp.concatenate([array[start : start + tile_count] for start in starts], axis=0)

    parts = []
    for green, cross in zip(greens, crosses):
        left, right = lax.select(member == 0, cross, green), lax.select(member == 0, green, cross)
        left = lax.select(to_core == 0, rows_of(left, 0), rows_of(left, 1))
        by_re, by_im = dot_rows(left, right[:order]), dot_rows(left, right[order:])
        parts.append((by_re[:half] + by_im[half:]).astype(jnp.bfloat16))
        parts.append(((by_re[half:] - by_im[:half]) * conj).astype(jnp.bfloat16))
    for side in range(2):
        out_ref[side * half : (side + 1) * half] = jnp.concatenate(
            [part[:, side * half : (side + 1) * half] for part in parts], axis=1
        )


def triple_kernel(
    retarded_ref, self_energy_ref, energy_ref, away_ref, green_ref, cross_ref, energy_out_ref, sigma_ref, sems, *, sizes
):
    energies, _, order, _ = green_ref.shape
    momentum, core = lax.axis_index("pair"), lax.axis_index("core")
    copies = []
    for e in range(energies):
        copies.append(pltpu.make_async_copy(retarded_ref.at[momentum, e], green_ref.at[e], sems.at[e, 0]))
        copies.append(pltpu.make_async_copy(self_energy_ref.at[0, e], sigma_ref.at[e], sems.at[e, 1]))
    copies.append(pltpu.make_async_copy(energy_ref, energy_out_ref, sems.at[energies, 0]))
    for copy in copies:
        copy.start()
    for copy in copies:
        copy.wait()
    greens = [green_ref[e].reshape(2 * order, order) for e in range(energies)]
    first = [[dot(greens[e], sigma_ref[e, part]) for part in range(2)] for e in range(energies)]
    crosses = [
        jnp.concatenate([by_re[:order] - by_im[order:], by_im[:order] + by_re[order:]], axis=0).astype(jnp.bfloat16)
        for by_re, by_im in first
    ]
    for e in range(energies):
        cross_ref[e] = crosses[e]
    write_blocks(away_ref, greens, crosses, 1 - core, sizes)


def arrange_kernel(
    green_ref, cross_ref, energy_ref, table_ref, own_ref, out_ref, back_ref, pick_ref, forward_ref, sems, *, sizes
):
    tile_count, hop_count = sizes
    count = pick_ref.shape[0]
    energies = count // (2 * tile_count * hop_count)
    devices = count // energies
    core = lax.axis_index("core")
    rows = table_ref.shape[0] // 2
    forward_copy = pltpu.make_async_copy(table_ref.at[pl.ds(0, rows)], forward_ref, sems.at[0])
    back_copy = pltpu.make_async_copy(table_ref.at[pl.ds(rows, rows)], back_ref, sems.at[1])
    forward_copy.start()
    back_copy.start()
    both = range(green_ref.shape[0])
    greens = [green_ref[e].reshape(cross_ref.shape[1:]) for e in both]
    write_blocks(own_ref, greens, [cross_ref[e] for e in both], core, sizes)
    slots = jnp.concatenate([energy_ref[r : r + 1] for r in range(energy_ref.shape[0])], axis=1)
    digit = lax.broadcasted_iota(jnp.int32, (16, count), 0)
    digits = jnp.where(digit == 0, slots >> 1, slots & 1).astype(jnp.float32).astype(jnp.bfloat16)
    column = lax.broadcasted_iota(jnp.int32, (1, count), 1)
    energy = sum((jnp.where(column >= n * devices, 1, 0) for n in range(1, energies)), jnp.zeros_like(column))
    device = column - energy * devices
    side, place = device & 1, device >> 1
    hop = sum((jnp.where(place >= n * tile_count, 1, 0) for n in range(1, hop_count)), jnp.zeros_like(column))
    place = (place - hop * tile_count) * hop_count + hop
    wanted = (place * 2 + side + core - 2 * side * core) * energies + energy
    row = lax.broadcasted_iota(jnp.int32, (count, count), 0)
    taken = dot(digits, one_hot(row == wanted))
    pick_ref[...] = one_hot(row == (2.0 * taken[:1] + taken[1:2]).astype(jnp.int32))
    forward_copy.wait()
    out_ref[...] = dot(forward_ref[...], pick_ref[...]).astype(jnp.bfloat16)
    back_copy.wait()


def times(left, right):
    return left[0] * right[0] - left[1] * right[1], left[0] * right[1] + left[1] * right[0]


def correlate_kernel(signal_ref, forward_ref, back_ref, out_ref, staged_ref):
    _, count, _ = staged_ref.shape
    devices = signal_ref.shape[0] // 2
    energies = count // devices
    half = signal_ref.shape[1] // (2 * energies)
    staged_ref[...] = jnp.zeros(staged_ref.shape, staged_ref.dtype)
    for component in range(2):
        signal = signal_ref[component * devices : (component + 1) * devices]
        for e in range(energies):
            for part in range(2):
                start = (2 * e + part) * half
                staged_ref[component, e * devices : (e + 1) * devices, part * LANES : part * LANES + half] = signal[
                    :, start : start + half
                ]
    spectra = []
    for component in range(2):
        cos_sum, sin_sum = (dot(forward_ref[r * count : (r + 1) * count], staged_ref[component]) for r in range(2))
        turned = (sin_sum[:, LANES:], -sin_sum[:, :LANES])
        plain = (cos_sum[:, :LANES], cos_sum[:, LANES:])
        spectra.append([[p + t for p, t in zip(plain, turned)], [p - t for p, t in zip(plain, turned)]])
    one, two = spectra
    ahead, behind = times(one[0], two[1]), times(one[1], two[0])
    even_parts = [ahead[0] + behind[0], ahead[1] + behind[1]]
    odd_parts = [behind[1] - ahead[1], ahead[0] - behind[0]]
    even = dot(back_ref[:count], jnp.concatenate(even_parts, axis=1).astype(jnp.bfloat16))
    odd = dot(back_ref[count:], jnp.concatenate(odd_parts, axis=1).astype(jnp.bfloat16))
    rows = count // 2
    for component, total in enumerate((even + odd, even - odd)):
        total = total.astype(out_ref.dtype)
        im, re = total[:, LANES : LANES + half], total[:, :half]
        out_ref[component] = jnp.concatenate([im[:rows], re[:rows], im[rows:], re[rows:]], axis=1)


def place_kernel(gathered_ref, out_ref, placed_ref, sems, *, scale):
    _, lags, _, tiles, order = out_ref.shape
    half, low = order // 2, lags // 2
    rows = low * tiles
    target = lax.broadcasted_iota(jnp.int32, (rows, rows), 0)
    source = lax.broadcasted_iota(jnp.int32, (rows, rows), 1)
    pick = one_hot((source & (low - 1)) * tiles + (source >> (low.bit_length() - 1)) == target)
    copies = []
    for high in range(2):
        for part in range(2):
            lane = (2 * high + part) * half
            both = [gathered_ref[side * rows : (side + 1) * rows, lane : lane + half] for side in range(2)]
            moved = dot(pick, jnp.concatenate(both, axis=1)) * (-scale if part else scale)
            for lag in range(low):
                placed_ref[high, part, lag] = moved[lag * tiles : (lag + 1) * tiles]
            copies.append(
                pltpu.make_async_copy(
                    placed_ref.at[high, part], out_ref.at[0, pl.ds(high * low, low), part], sems.at[high, part]
                )
            )
            copies[-1].start()
    for copy in copies:
        copy.wait()


def on_chip(array):
    return pltpu.with_memory_space_constraint(array, pltpu.VMEM) if not INTERPRET else array


def off_chip(array):
    return pltpu.with_memory_space_constraint(array, pltpu.HBM) if not INTERPRET else array


def on_chip_out(shape, dtype):
    return pltpu.VMEM(shape, dtype) if not INTERPRET else jax.ShapeDtypeStruct(shape, dtype)


def body(retarded, self_energy, energy_of, *, sizes):
    tile_count, hop_count = sizes
    energies, order = retarded.shape[1], retarded.shape[3]
    half = order // 2
    slot_count = energy_of.shape[0]
    in_vmem = pl.BlockSpec(memory_space=pltpu.VMEM)
    in_place = pl.BlockSpec(memory_space=pl.ANY)
    cos_part, sin_part = twiddles(slot_count)
    lag_count = slot_count // tile_count
    lags = np.arange(slot_count).reshape(tile_count, 2, lag_count // 2).transpose(1, 0, 2).reshape(-1)
    table = jnp.asarray(np.concatenate([cos_part, sin_part, cos_part.T[lags], sin_part.T[lags]]), jnp.bfloat16)
    lanes = math.gcd(slot_count, LANES)
    slot_energy = energy_of.reshape(slot_count // lanes, lanes)
    block = on_chip_out((order, 2 * energies * half), jnp.bfloat16)
    greens = on_chip_out((energies, 2, order, order), jnp.bfloat16)
    crosses = on_chip_out((energies, 2 * order, order), jnp.bfloat16)
    away, green, cross, slot_energy = pl.pallas_call(
        functools.partial(triple_kernel, sizes=sizes),
        out_shape=(block, greens, crosses, on_chip_out(slot_energy.shape, jnp.int32)),
        in_specs=[in_place] * 3,
        out_specs=(in_vmem,) * 4,
        scratch_shapes=[
            pltpu.VMEM((energies, 2, order, order), jnp.bfloat16),
            pltpu.SemaphoreType.DMA((energies + 1, 2)),
        ],
        compiler_params=SCHEDULE,
        interpret=INTERPRET,
        name="triple",
    )(*(off_chip(array) for array in (retarded, self_energy, slot_energy)))
    sibling = lax.ppermute(away, "core", [(0, 1), (1, 0)])
    tables = on_chip_out((2 * slot_count, slot_count), jnp.bfloat16)
    own, forward, back = pl.pallas_call(
        functools.partial(arrange_kernel, sizes=sizes),
        out_shape=(block, tables, tables),
        in_specs=[in_vmem] * 3 + [in_place],
        out_specs=(in_vmem,) * 3,
        scratch_shapes=[
            pltpu.VMEM((slot_count, slot_count), jnp.bfloat16),
            pltpu.VMEM((2 * slot_count, slot_count), jnp.bfloat16),
            pltpu.SemaphoreType.DMA((2,)),
        ],
        compiler_params=SCHEDULE,
        interpret=INTERPRET,
        name="arrange",
    )(on_chip(green), on_chip(cross), on_chip(slot_energy), off_chip(table))
    blocks, forward = lax.optimization_barrier((jnp.stack([own, sibling], axis=1), forward))
    gathered = lax.all_to_all(blocks, ("mem", "zh", "tile"), split_axis=0, concat_axis=0, tiled=True)
    polar = pl.pallas_call(
        correlate_kernel,
        out_shape=on_chip_out((2, slot_count // 2, 4 * half), jnp.bfloat16),
        in_specs=[in_vmem] * 3,
        out_specs=in_vmem,
        scratch_shapes=[pltpu.VMEM((2, slot_count, 2 * LANES), jnp.bfloat16)],
        compiler_params=PLAIN,
        interpret=INTERPRET,
        name="correlate",
    )(on_chip(gathered.reshape(2 * order, 2 * energies * half)), on_chip(forward), on_chip(back))
    packed = polar.reshape(2 * tile_count, lag_count // 2, 4 * half)
    regrouped = lax.all_to_all(packed, ("mem", "tile"), split_axis=0, concat_axis=0, tiled=True)
    return pl.pallas_call(
        functools.partial(place_kernel, scale=1.0 / (2 * slot_count * math.sqrt(slot_count))),
        out_shape=jax.ShapeDtypeStruct((1, lag_count, 2, tile_count, order), jnp.float32),
        in_specs=[in_vmem],
        out_specs=in_place,
        scratch_shapes=[
            pltpu.VMEM((2, 2, lag_count // 2, tile_count, order), jnp.float32),
            pltpu.SemaphoreType.DMA((2, 2)),
        ],
        compiler_params=SCHEDULE,
        interpret=INTERPRET,
        name="place",
    )(on_chip(regrouped.reshape(tile_count * lag_count, 4 * half)))


def solution(mesh):
    comp, tile, rep = mesh.devices.shape
    split = Mesh(mesh.devices.reshape(2, comp // 2, tile, rep // 2, 2), ("pair", "mem", "tile", "zh", "core"))
    energy_axes = ("tile", "zh", "core")
    placed = (
        P(None, energy_axes, None, None, None),
        P(("pair", "mem"), energy_axes, None, None, None),
        P(),
    )
    return jax.shard_map(
        functools.partial(body, sizes=(tile, rep // 2)),
        mesh=split,
        in_specs=placed,
        out_specs=P(("pair", "mem"), "tile", None, ("zh", "core"), None),
        check_vma=False,
    )
```

```python
import functools
import math

import jax
import jax.numpy as jnp
import numpy as np
from jax import lax
from jax.experimental import pallas as pl
from jax.experimental.pallas import tpu as pltpu
from jax.sharding import Mesh, PartitionSpec as P

LANES = 128
INTERPRET = False
CHUNKS = 2
GRANT = 16 * 2**20
PLAIN = pltpu.CompilerParams(vmem_limit_bytes=GRANT)
SCHEDULE = pltpu.CompilerParams(vmem_limit_bytes=GRANT)


def twiddles(count):
    steps = (2 * np.arange(count)[:, None] + 1) * np.arange(count)[None, :] % (4 * count)
    angles = steps * (math.pi / (2 * count))
    return np.cos(angles), np.sin(angles)


def dot(left_side, right_side):
    return jnp.dot(left_side, right_side, preferred_element_type=jnp.float32)


def dot_rows(left_side, right_side):
    return lax.dot_general(left_side, right_side, (((1,), (1,)), ((), ())), preferred_element_type=jnp.float32)


def one_hot(condition):
    return jnp.where(condition, 1.0, 0.0).astype(jnp.bfloat16)


def packed(parts):
    third = parts[3].shape[1] // 3
    return jnp.concatenate(
        [piece for n in range(3) for piece in (parts[n], parts[3][:, n * third : (n + 1) * third])], axis=1
    )


def piece(array, n):
    pitch = array.shape[1] // 3
    half = 3 * pitch // 4
    if n < 3:
        return array[:, n * pitch : n * pitch + half]
    return jnp.concatenate([array[:, m * pitch + half : (m + 1) * pitch] for m in range(3)], axis=1)


def write_blocks(out_ref, greens, crosses, to_core, sizes):
    tile_count, hop_count = sizes
    order = greens[0].shape[1]
    half = order // 2
    member = lax.axis_index("mem")
    conj = jnp.where(member == 0, 1.0, -1.0)

    def rows_of(array, core):
        starts = [part * order + (2 * hop + core) * tile_count for part in range(2) for hop in range(hop_count)]
        return jnp.concatenate([array[start : start + tile_count] for start in starts], axis=0)

    parts = []
    for green, cross in zip(greens, crosses):
        left, right = lax.select(member == 0, cross, green), lax.select(member == 0, green, cross)
        left = lax.select(to_core == 0, rows_of(left, 0), rows_of(left, 1))
        by_re, by_im = dot_rows(left, right[:order]), dot_rows(left, right[order:])
        parts.append((by_re[:half] + by_im[half:]).astype(jnp.bfloat16))
        parts.append(((by_re[half:] - by_im[:half]) * conj).astype(jnp.bfloat16))
    for side in range(2):
        out_ref[side * half : (side + 1) * half] = packed([part[:, side * half : (side + 1) * half] for part in parts])


def triple_kernel(
    retarded_ref, self_energy_ref, energy_ref, table_ref, away_ref, green_ref, cross_ref, energy_out_ref, table_out_ref,
    sigma_ref, sems, *, sizes
):
    energies, _, order, _ = green_ref.shape
    momentum, core = lax.axis_index("pair"), lax.axis_index("core")
    copies = []
    for e in range(energies):
        for part in range(2):
            source, target = retarded_ref.at[momentum, e, part], green_ref.at[e, part]
            copies.append(pltpu.make_async_copy(source, target, sems.at[e, part]))
            source, target = self_energy_ref.at[0, e, part], sigma_ref.at[e, part]
            copies.append(pltpu.make_async_copy(source, target, sems.at[e, 2 + part]))
    later = (
        pltpu.make_async_copy(energy_ref, energy_out_ref, sems.at[energies, 0]),
        pltpu.make_async_copy(table_ref, table_out_ref, sems.at[energies, 1]),
    )
    for copy in (*copies, *later):
        copy.start()
    for copy in copies:
        copy.wait()
    greens = [green_ref[e].reshape(2 * order, order) for e in range(energies)]
    first = [[dot(greens[e], sigma_ref[e, part]) for part in range(2)] for e in range(energies)]
    crosses = [
        jnp.concatenate([by_re[:order] - by_im[order:], by_im[:order] + by_re[order:]], axis=0).astype(jnp.bfloat16)
        for by_re, by_im in first
    ]
    for e in range(energies):
        cross_ref[e] = crosses[e]
    write_blocks(away_ref, greens, crosses, 1 - core, sizes)
    for copy in later:
        copy.wait()


def arrange_kernel(green_ref, cross_ref, energy_ref, table_ref, own_ref, out_ref, pick_ref, *, sizes):
    tile_count, hop_count = sizes
    count = pick_ref.shape[0]
    energies = count // (2 * tile_count * hop_count)
    devices = count // energies
    core = lax.axis_index("core")
    both = range(green_ref.shape[0])
    greens = [green_ref[e].reshape(cross_ref.shape[1:]) for e in both]
    write_blocks(own_ref, greens, [cross_ref[e] for e in both], core, sizes)
    slots = jnp.concatenate([energy_ref[r : r + 1] for r in range(energy_ref.shape[0])], axis=1)
    digit = lax.broadcasted_iota(jnp.int32, (16, count), 0)
    digits = jnp.where(digit == 0, slots >> 1, slots & 1).astype(jnp.float32).astype(jnp.bfloat16)
    column = lax.broadcasted_iota(jnp.int32, (1, count), 1)
    energy = sum((jnp.where(column >= n * devices, 1, 0) for n in range(1, energies)), jnp.zeros_like(column))
    device = column - energy * devices
    side, place = device & 1, device >> 1
    hop = sum((jnp.where(place >= n * tile_count, 1, 0) for n in range(1, hop_count)), jnp.zeros_like(column))
    place = (place - hop * tile_count) * hop_count + hop
    wanted = (place * 2 + side + core - 2 * side * core) * energies + energy
    row = lax.broadcasted_iota(jnp.int32, (count, count), 0)
    taken = dot(digits, one_hot(row == wanted))
    pick_ref[...] = one_hot(row == (2.0 * taken[:1] + taken[1:2]).astype(jnp.int32))
    out_ref[...] = dot(table_ref[: 2 * count], pick_ref[...]).astype(jnp.bfloat16)


def times(left, right):
    return left[0] * right[0] - left[1] * right[1], left[0] * right[1] + left[1] * right[0]


def correlate_kernel(signal_ref, forward_ref, table_ref, out_ref, staged_ref):
    _, count, _ = staged_ref.shape
    devices = signal_ref.shape[0] // 2
    energies = count // devices
    half = signal_ref.shape[1] // (2 * energies)
    gap = jnp.zeros((devices, LANES - half), staged_ref.dtype)
    for component in range(2):
        signal = signal_ref[component * devices : (component + 1) * devices]
        for e in range(energies):
            for part in range(2):
                staged_ref[component, e * devices : (e + 1) * devices, part * LANES : (part + 1) * LANES] = jnp.concatenate(
                    [piece(signal, 2 * e + part), gap], axis=1
                )
    spectra = []
    for component in range(2):
        cos_sum, sin_sum = (dot(forward_ref[r * count : (r + 1) * count], staged_ref[component]) for r in range(2))
        turned = (sin_sum[:, LANES:], -sin_sum[:, :LANES])
        plain = (cos_sum[:, :LANES], cos_sum[:, LANES:])
        spectra.append([[p + t for p, t in zip(plain, turned)], [p - t for p, t in zip(plain, turned)]])
    one, two = spectra
    ahead, behind = times(one[0], two[1]), times(one[1], two[0])
    even_parts = [ahead[0] + behind[0], ahead[1] + behind[1]]
    odd_parts = [behind[1] - ahead[1], ahead[0] - behind[0]]
    even_parts = jnp.concatenate(even_parts, axis=1).astype(jnp.bfloat16)
    odd_parts = jnp.concatenate(odd_parts, axis=1).astype(jnp.bfloat16)
    size = count // CHUNKS
    rows = size // 2
    for n in range(CHUNKS):
        even = dot(table_ref[2 * count + n * size : 2 * count + (n + 1) * size], even_parts)
        odd = dot(table_ref[3 * count + n * size : 3 * count + (n + 1) * size], odd_parts)
        for component, total in enumerate((even + odd, even - odd)):
            total = total.astype(out_ref.dtype)
            im, re = total[:, LANES : LANES + half], total[:, :half]
            out_ref[component, n * rows : (n + 1) * rows] = packed([im[:rows], re[:rows], im[rows:], re[rows:]])


def place_kernel(gathered_ref, out_ref, placed_ref, sems, *, scale):
    _, lags, _, tiles, order = out_ref.shape
    half, low = order // 2, lags // 2
    rows = low * tiles
    target = lax.broadcasted_iota(jnp.int32, (rows, rows), 0)
    source = lax.broadcasted_iota(jnp.int32, (rows, rows), 1)
    pick = one_hot((source & (low - 1)) * tiles + (source >> (low.bit_length() - 1)) == target)
    copies = []
    for high in range(2):
        for part in range(2):
            both = [piece(gathered_ref[side * rows : (side + 1) * rows], 2 * high + part) for side in range(2)]
            moved = dot(pick, jnp.concatenate(both, axis=1)) * (-scale if part else scale)
            for lag in range(low):
                placed_ref[high, part, lag] = moved[lag * tiles : (lag + 1) * tiles]
            copies.append(
                pltpu.make_async_copy(
                    placed_ref.at[high, part], out_ref.at[0, pl.ds(high * low, low), part], sems.at[high, part]
                )
            )
            copies[-1].start()
    for copy in copies:
        copy.wait()


def on_chip(array):
    return pltpu.with_memory_space_constraint(array, pltpu.VMEM) if not INTERPRET else array


def off_chip(array):
    return pltpu.with_memory_space_constraint(array, pltpu.HBM) if not INTERPRET else array


def on_chip_out(shape, dtype):
    return pltpu.VMEM(shape, dtype) if not INTERPRET else jax.ShapeDtypeStruct(shape, dtype)


def body(retarded, self_energy, energy_of, *, sizes):
    tile_count, hop_count = sizes
    energies, order = retarded.shape[1], retarded.shape[3]
    half = order // 2
    slot_count = energy_of.shape[0]
    in_vmem = pl.BlockSpec(memory_space=pltpu.VMEM)
    in_place = pl.BlockSpec(memory_space=pl.ANY)
    cos_part, sin_part = twiddles(slot_count)
    lag_count = slot_count // tile_count
    lags = np.arange(slot_count).reshape(tile_count, 2, lag_count // 2).transpose(1, 0, 2).reshape(-1)
    lags = lags.reshape(2, CHUNKS, -1).transpose(1, 0, 2).reshape(-1)
    table = jnp.asarray(np.concatenate([cos_part, sin_part, cos_part.T[lags], sin_part.T[lags]]), jnp.bfloat16)
    lanes = math.gcd(slot_count, LANES)
    slot_energy = energy_of.reshape(slot_count // lanes, lanes)
    block = on_chip_out((order, 2 * energies * half), jnp.bfloat16)
    greens = on_chip_out((energies, 2, order, order), jnp.bfloat16)
    crosses = on_chip_out((energies, 2 * order, order), jnp.bfloat16)
    away, green, cross, slot_energy, table = pl.pallas_call(
        functools.partial(triple_kernel, sizes=sizes),
        out_shape=(
            block,
            greens,
            crosses,
            on_chip_out(slot_energy.shape, jnp.int32),
            on_chip_out(table.shape, jnp.bfloat16),
        ),
        in_specs=[in_place] * 4,
        out_specs=(in_vmem,) * 5,
        scratch_shapes=[
            pltpu.VMEM((energies, 2, order, order), jnp.bfloat16),
            pltpu.SemaphoreType.DMA((energies + 1, 4)),
        ],
        compiler_params=SCHEDULE,
        interpret=INTERPRET,
        name="triple",
    )(*(off_chip(array) for array in (retarded, self_energy, slot_energy, table)))
    sibling = lax.ppermute(away, "core", [(0, 1), (1, 0)])
    own, forward = pl.pallas_call(
        functools.partial(arrange_kernel, sizes=sizes),
        out_shape=(block, on_chip_out((2 * slot_count, slot_count), jnp.bfloat16)),
        in_specs=[in_vmem] * 4,
        out_specs=(in_vmem,) * 2,
        scratch_shapes=[pltpu.VMEM((slot_count, slot_count), jnp.bfloat16)],
        compiler_params=SCHEDULE,
        interpret=INTERPRET,
        name="arrange",
    )(on_chip(green), on_chip(cross), on_chip(slot_energy), on_chip(table))
    blocks, forward = lax.optimization_barrier((jnp.stack([own, sibling], axis=1), forward))
    gathered = lax.all_to_all(blocks, ("mem", "zh", "tile"), split_axis=0, concat_axis=0, tiled=True)
    polar = pl.pallas_call(
        correlate_kernel,
        out_shape=on_chip_out((2, slot_count // 2, 4 * half), jnp.bfloat16),
        in_specs=[in_vmem] * 3,
        out_specs=in_vmem,
        scratch_shapes=[pltpu.VMEM((2, slot_count, 2 * LANES), jnp.bfloat16)],
        compiler_params=SCHEDULE,
        interpret=INTERPRET,
        name="correlate",
    )(on_chip(gathered.reshape(2 * order, 2 * energies * half)), on_chip(forward), on_chip(table))
    packed = polar.reshape(2 * tile_count, lag_count // 2, 4 * half)
    regrouped = lax.all_to_all(packed, ("mem", "tile"), split_axis=0, concat_axis=0, tiled=True)
    return pl.pallas_call(
        functools.partial(place_kernel, scale=1.0 / (2 * slot_count * math.sqrt(slot_count))),
        out_shape=jax.ShapeDtypeStruct((1, lag_count, 2, tile_count, order), jnp.float32),
        in_specs=[in_vmem],
        out_specs=in_place,
        scratch_shapes=[
            pltpu.VMEM((2, 2, lag_count // 2, tile_count, order), jnp.float32),
            pltpu.SemaphoreType.DMA((2, 2)),
        ],
        compiler_params=SCHEDULE,
        interpret=INTERPRET,
        name="place",
    )(on_chip(regrouped.reshape(tile_count * lag_count, 4 * half)))


def solution(mesh):
    comp, tile, rep = mesh.devices.shape
    split = Mesh(mesh.devices.reshape(2, comp // 2, tile, rep // 2, 2), ("pair", "mem", "tile", "zh", "core"))
    energy_axes = ("tile", "zh", "core")
    placed = (
        P(None, energy_axes, None, None, None),
        P(("pair", "mem"), energy_axes, None, None, None),
        P(),
    )
    return jax.shard_map(
        functools.partial(body, sizes=(tile, rep // 2)),
        mesh=split,
        in_specs=placed,
        out_specs=P(("pair", "mem"), "tile", None, ("zh", "core"), None),
        check_vma=False,
    )
```

```python
import functools
import math

import jax
import jax.numpy as jnp
import numpy as np
from jax import lax
from jax.experimental import pallas as pl
from jax.experimental.pallas import tpu as pltpu
from jax.sharding import Mesh, PartitionSpec as P

LANES = 128
INTERPRET = False
RUN = 3
CHUNKS = 2
GRANT = 16 * 2**20
PLAIN = pltpu.CompilerParams(vmem_limit_bytes=GRANT)
SCHEDULE = pltpu.CompilerParams(vmem_limit_bytes=GRANT)


def twiddles(count):
    steps = (2 * np.arange(count)[:, None] + 1) * np.arange(count)[None, :] % (4 * count)
    angles = steps * (math.pi / (2 * count))
    return np.cos(angles), np.sin(angles)


def dot(left_side, right_side):
    return jnp.dot(left_side, right_side, preferred_element_type=jnp.float32)


def dot_rows(left_side, right_side):
    return lax.dot_general(left_side, right_side, (((1,), (1,)), ((), ())), preferred_element_type=jnp.float32)


def one_hot(condition):
    return jnp.where(condition, 1.0, 0.0).astype(jnp.bfloat16)


def packed(parts):
    third = parts[3].shape[1] // 3
    return jnp.concatenate(
        [piece for n in range(3) for piece in (parts[n], parts[3][:, n * third : (n + 1) * third])], axis=1
    )


def piece(array, n):
    pitch = array.shape[1] // 3
    half = 3 * pitch // 4
    if n < 3:
        return array[:, n * pitch : n * pitch + half]
    return jnp.concatenate([array[:, m * pitch + half : (m + 1) * pitch] for m in range(3)], axis=1)


def write_blocks(out_ref, greens, crosses, to_core, sizes):
    tile_count, hop_count = sizes
    order = greens[0].shape[1]
    half = order // 2
    member = lax.axis_index("mem")
    conj = jnp.where(member == 0, 1.0, -1.0)

    def rows_of(array, core):
        starts = [part * order + (2 * hop + core) * tile_count for part in range(2) for hop in range(hop_count)]
        return jnp.concatenate([array[start : start + tile_count] for start in starts], axis=0)

    parts = []
    for green, cross in zip(greens, crosses):
        left, right = lax.select(member == 0, cross, green), lax.select(member == 0, green, cross)
        left = lax.select(to_core == 0, rows_of(left, 0), rows_of(left, 1))
        by_re, by_im = dot_rows(left, right[:order]), dot_rows(left, right[order:])
        parts.append((by_re[:half] + by_im[half:]).astype(jnp.bfloat16))
        parts.append(((by_re[half:] - by_im[:half]) * conj).astype(jnp.bfloat16))
    for side in range(2):
        out_ref[side * half : (side + 1) * half] = packed([part[:, side * half : (side + 1) * half] for part in parts])


def triple_kernel(
    retarded_ref, self_energy_ref, energy_ref, table_ref, away_ref, green_ref, cross_ref, energy_out_ref, table_out_ref,
    sigma_ref, sems, *, sizes
):
    energies, _, order, _ = green_ref.shape
    momentum, core = lax.axis_index("pair"), lax.axis_index("core")
    copies = []
    for e in range(energies):
        for part in range(2):
            source, target = retarded_ref.at[momentum, e, part], green_ref.at[e, part]
            copies.append(pltpu.make_async_copy(source, target, sems.at[e, part]))
            source, target = self_energy_ref.at[0, e, part], sigma_ref.at[e, part]
            copies.append(pltpu.make_async_copy(source, target, sems.at[e, 2 + part]))
    later = (
        pltpu.make_async_copy(energy_ref, energy_out_ref, sems.at[energies, 0]),
        pltpu.make_async_copy(table_ref, table_out_ref, sems.at[energies, 1]),
    )
    for copy in (*copies, *later):
        copy.start()
    for copy in copies:
        copy.wait()
    greens = [green_ref[e].reshape(2 * order, order) for e in range(energies)]
    first = [[dot(greens[e], sigma_ref[e, part]) for part in range(2)] for e in range(energies)]
    crosses = [
        jnp.concatenate([by_re[:order] - by_im[order:], by_im[:order] + by_re[order:]], axis=0).astype(jnp.bfloat16)
        for by_re, by_im in first
    ]
    for e in range(energies):
        cross_ref[e] = crosses[e]
    write_blocks(away_ref, greens, crosses, 1 - core, sizes)
    for copy in later:
        copy.wait()


def arrange_kernel(green_ref, cross_ref, energy_ref, table_ref, own_ref, out_ref, pick_ref, *, sizes):
    tile_count, hop_count = sizes
    count = pick_ref.shape[0]
    energies = count // (2 * tile_count * hop_count)
    devices = count // energies
    core = lax.axis_index("core")
    both = range(green_ref.shape[0])
    greens = [green_ref[e].reshape(cross_ref.shape[1:]) for e in both]
    write_blocks(own_ref, greens, [cross_ref[e] for e in both], core, sizes)
    slots = jnp.concatenate([energy_ref[r : r + 1] for r in range(energy_ref.shape[0])], axis=1)
    digit = lax.broadcasted_iota(jnp.int32, (16, count), 0)
    digits = jnp.where(digit == 0, slots >> 1, slots & 1).astype(jnp.float32).astype(jnp.bfloat16)
    column = lax.broadcasted_iota(jnp.int32, (1, count), 1)
    energy = sum((jnp.where(column >= n * devices, 1, 0) for n in range(1, energies)), jnp.zeros_like(column))
    device = column - energy * devices
    side, place = device & 1, device >> 1
    hop = sum((jnp.where(place >= n * tile_count, 1, 0) for n in range(1, hop_count)), jnp.zeros_like(column))
    place = place - hop * tile_count
    across = tile_count // RUN
    place = ((place & (across - 1)) * RUN + (place >> (across.bit_length() - 1))) * hop_count + hop
    wanted = (place * 2 + side + core - 2 * side * core) * energies + energy
    row = lax.broadcasted_iota(jnp.int32, (count, count), 0)
    taken = dot(digits, one_hot(row == wanted))
    pick_ref[...] = one_hot(row == (2.0 * taken[:1] + taken[1:2]).astype(jnp.int32))
    out_ref[...] = dot(table_ref[: 2 * count], pick_ref[...]).astype(jnp.bfloat16)


def times(left, right):
    return left[0] * right[0] - left[1] * right[1], left[0] * right[1] + left[1] * right[0]


def correlate_kernel(signal_ref, forward_ref, table_ref, out_ref, staged_ref):
    _, count, _ = staged_ref.shape
    devices = signal_ref.shape[0] // 2
    energies = count // devices
    half = signal_ref.shape[1] // (2 * energies)
    gap = jnp.zeros((devices, LANES - half), staged_ref.dtype)
    for component in range(2):
        signal = signal_ref[component * devices : (component + 1) * devices]
        for e in range(energies):
            for part in range(2):
                staged_ref[component, e * devices : (e + 1) * devices, part * LANES : (part + 1) * LANES] = jnp.concatenate(
                    [piece(signal, 2 * e + part), gap], axis=1
                )
    spectra = []
    for component in range(2):
        cos_sum, sin_sum = (dot(forward_ref[r * count : (r + 1) * count], staged_ref[component]) for r in range(2))
        turned = (sin_sum[:, LANES:], -sin_sum[:, :LANES])
        plain = (cos_sum[:, :LANES], cos_sum[:, LANES:])
        spectra.append([[p + t for p, t in zip(plain, turned)], [p - t for p, t in zip(plain, turned)]])
    one, two = spectra
    ahead, behind = times(one[0], two[1]), times(one[1], two[0])
    even_parts = [ahead[0] + behind[0], ahead[1] + behind[1]]
    odd_parts = [behind[1] - ahead[1], ahead[0] - behind[0]]
    even_parts = jnp.concatenate(even_parts, axis=1).astype(jnp.bfloat16)
    odd_parts = jnp.concatenate(odd_parts, axis=1).astype(jnp.bfloat16)
    size = count // CHUNKS
    rows = size // 2
    for n in range(CHUNKS):
        even = dot(table_ref[2 * count + n * size : 2 * count + (n + 1) * size], even_parts)
        odd = dot(table_ref[3 * count + n * size : 3 * count + (n + 1) * size], odd_parts)
        for component, total in enumerate((even + odd, even - odd)):
            total = total.astype(out_ref.dtype)
            im, re = total[:, LANES : LANES + half], total[:, :half]
            out_ref[component, n * rows : (n + 1) * rows] = packed([im[:rows], re[:rows], im[rows:], re[rows:]])


def place_kernel(gathered_ref, out_ref, placed_ref, sems, *, scale):
    _, lags, _, tiles, order = out_ref.shape
    half, low = order // 2, lags // 2
    rows = low * tiles
    target = lax.broadcasted_iota(jnp.int32, (rows, rows), 0)
    source = lax.broadcasted_iota(jnp.int32, (rows, rows), 1)
    pick = one_hot((source & (low - 1)) * tiles + (source >> (low.bit_length() - 1)) == target)
    copies = []
    for high in range(2):
        for part in range(2):
            both = [piece(gathered_ref[side * rows : (side + 1) * rows], 2 * high + part) for side in range(2)]
            moved = dot(pick, jnp.concatenate(both, axis=1)) * (-scale if part else scale)
            for lag in range(low):
                placed_ref[high, part, lag] = moved[lag * tiles : (lag + 1) * tiles]
            copies.append(
                pltpu.make_async_copy(
                    placed_ref.at[high, part], out_ref.at[0, pl.ds(high * low, low), part], sems.at[high, part]
                )
            )
            copies[-1].start()
    for copy in copies:
        copy.wait()


def on_chip(array):
    return pltpu.with_memory_space_constraint(array, pltpu.VMEM) if not INTERPRET else array


def off_chip(array):
    return pltpu.with_memory_space_constraint(array, pltpu.HBM) if not INTERPRET else array


def on_chip_out(shape, dtype):
    return pltpu.VMEM(shape, dtype) if not INTERPRET else jax.ShapeDtypeStruct(shape, dtype)


def body(retarded, self_energy, energy_of, *, sizes):
    tile_count, hop_count = sizes
    energies, order = retarded.shape[1], retarded.shape[3]
    half = order // 2
    slot_count = energy_of.shape[0]
    in_vmem = pl.BlockSpec(memory_space=pltpu.VMEM)
    in_place = pl.BlockSpec(memory_space=pl.ANY)
    cos_part, sin_part = twiddles(slot_count)
    lag_count = slot_count // tile_count
    lags = np.arange(slot_count).reshape(tile_count // RUN, RUN, 2, lag_count // 2).transpose(2, 1, 0, 3).reshape(-1)
    lags = lags.reshape(2, CHUNKS, -1).transpose(1, 0, 2).reshape(-1)
    table = jnp.asarray(np.concatenate([cos_part, sin_part, cos_part.T[lags], sin_part.T[lags]]), jnp.bfloat16)
    lanes = math.gcd(slot_count, LANES)
    slot_energy = energy_of.reshape(slot_count // lanes, lanes)
    block = on_chip_out((order, 2 * energies * half), jnp.bfloat16)
    greens = on_chip_out((energies, 2, order, order), jnp.bfloat16)
    crosses = on_chip_out((energies, 2 * order, order), jnp.bfloat16)
    away, green, cross, slot_energy, table = pl.pallas_call(
        functools.partial(triple_kernel, sizes=sizes),
        out_shape=(
            block,
            greens,
            crosses,
            on_chip_out(slot_energy.shape, jnp.int32),
            on_chip_out(table.shape, jnp.bfloat16),
        ),
        in_specs=[in_place] * 4,
        out_specs=(in_vmem,) * 5,
        scratch_shapes=[
            pltpu.VMEM((energies, 2, order, order), jnp.bfloat16),
            pltpu.SemaphoreType.DMA((energies + 1, 4)),
        ],
        compiler_params=SCHEDULE,
        interpret=INTERPRET,
        name="triple",
    )(*(off_chip(array) for array in (retarded, self_energy, slot_energy, table)))
    sibling = lax.ppermute(away, "core", [(0, 1), (1, 0)])
    own, forward = pl.pallas_call(
        functools.partial(arrange_kernel, sizes=sizes),
        out_shape=(block, on_chip_out((2 * slot_count, slot_count), jnp.bfloat16)),
        in_specs=[in_vmem] * 4,
        out_specs=(in_vmem,) * 2,
        scratch_shapes=[pltpu.VMEM((slot_count, slot_count), jnp.bfloat16)],
        compiler_params=SCHEDULE,
        interpret=INTERPRET,
        name="arrange",
    )(on_chip(green), on_chip(cross), on_chip(slot_energy), on_chip(table))
    blocks, forward = lax.optimization_barrier((jnp.stack([own, sibling], axis=1), forward))
    gathered = lax.all_to_all(blocks, ("mem", "zh", "run", "across"), split_axis=0, concat_axis=0, tiled=True)
    polar = pl.pallas_call(
        correlate_kernel,
        out_shape=on_chip_out((2, slot_count // 2, 4 * half), jnp.bfloat16),
        in_specs=[in_vmem] * 3,
        out_specs=in_vmem,
        scratch_shapes=[pltpu.VMEM((2, slot_count, 2 * LANES), jnp.bfloat16)],
        compiler_params=SCHEDULE,
        interpret=INTERPRET,
        name="correlate",
    )(on_chip(gathered.reshape(2 * order, 2 * energies * half)), on_chip(forward), on_chip(table))
    packed = polar.reshape(2 * tile_count, lag_count // 2, 4 * half)
    regrouped = lax.all_to_all(packed, ("mem", "run", "across"), split_axis=0, concat_axis=0, tiled=True)
    return pl.pallas_call(
        functools.partial(place_kernel, scale=1.0 / (2 * slot_count * math.sqrt(slot_count))),
        out_shape=jax.ShapeDtypeStruct((1, lag_count, 2, tile_count, order), jnp.float32),
        in_specs=[in_vmem],
        out_specs=in_place,
        scratch_shapes=[
            pltpu.VMEM((2, 2, lag_count // 2, tile_count, order), jnp.float32),
            pltpu.SemaphoreType.DMA((2, 2)),
        ],
        compiler_params=SCHEDULE,
        interpret=INTERPRET,
        name="place",
    )(on_chip(regrouped.reshape(tile_count * lag_count, 4 * half)))


def solution(mesh):
    comp, tile, rep = mesh.devices.shape
    split = Mesh(
        mesh.devices.reshape(2, comp // 2, tile // RUN, RUN, rep // 2, 2),
        ("pair", "mem", "across", "run", "zh", "core"),
    )
    energy_axes = ("across", "run", "zh", "core")
    placed = (
        P(None, energy_axes, None, None, None),
        P(("pair", "mem"), energy_axes, None, None, None),
        P(),
    )
    return jax.shard_map(
        functools.partial(body, sizes=(tile, rep // 2)),
        mesh=split,
        in_specs=placed,
        out_specs=P(("pair", "mem"), ("across", "run"), None, ("zh", "core"), None),
        check_vma=False,
    )
```

```python
import functools
import math

import jax
import jax.numpy as jnp
import numpy as np
from jax import lax
from jax.experimental import pallas as pl
from jax.experimental.pallas import tpu as pltpu
from jax.sharding import Mesh, PartitionSpec as P

LANES = 128
INTERPRET = False
CHUNKS = 2
GRANT = 16 * 2**20
PLAIN = pltpu.CompilerParams(vmem_limit_bytes=GRANT)
SCHEDULE = pltpu.CompilerParams(vmem_limit_bytes=GRANT)


def twiddles(count):
    steps = (2 * np.arange(count)[:, None] + 1) * np.arange(count)[None, :] % (4 * count)
    angles = steps * (math.pi / (2 * count))
    return np.cos(angles), np.sin(angles)


def dot(left_side, right_side):
    return jnp.dot(left_side, right_side, preferred_element_type=jnp.float32)


def dot_rows(left_side, right_side):
    return lax.dot_general(left_side, right_side, (((1,), (1,)), ((), ())), preferred_element_type=jnp.float32)


def one_hot(condition):
    return jnp.where(condition, 1.0, 0.0).astype(jnp.bfloat16)


def packed(parts):
    third = parts[3].shape[1] // 3
    return jnp.concatenate(
        [piece for n in range(3) for piece in (parts[n], parts[3][:, n * third : (n + 1) * third])], axis=1
    )


def piece(array, n):
    pitch = array.shape[1] // 3
    half = 3 * pitch // 4
    if n < 3:
        return array[:, n * pitch : n * pitch + half]
    return jnp.concatenate([array[:, m * pitch + half : (m + 1) * pitch] for m in range(3)], axis=1)


def write_blocks(out_ref, greens, crosses, to_core, sizes):
    tile_count, hop_count = sizes
    order = greens[0].shape[1]
    half = order // 2
    member = lax.axis_index("mem")
    conj = jnp.where(member == 0, 1.0, -1.0)

    def rows_of(array, core):
        starts = [part * order + (2 * hop + core) * tile_count for part in range(2) for hop in range(hop_count)]
        return jnp.concatenate([array[start : start + tile_count] for start in starts], axis=0)

    parts = []
    for green, cross in zip(greens, crosses):
        left, right = lax.select(member == 0, cross, green), lax.select(member == 0, green, cross)
        left = lax.select(to_core == 0, rows_of(left, 0), rows_of(left, 1))
        by_re, by_im = dot_rows(left, right[:order]), dot_rows(left, right[order:])
        parts.append((by_re[:half] + by_im[half:]).astype(jnp.bfloat16))
        parts.append(((by_re[half:] - by_im[:half]) * conj).astype(jnp.bfloat16))
    for side in range(2):
        out_ref[side * half : (side + 1) * half] = packed([part[:, side * half : (side + 1) * half] for part in parts])


def triple_kernel(
    retarded_ref, self_energy_ref, energy_ref, table_ref, away_ref, green_ref, cross_ref, energy_out_ref, table_out_ref,
    sigma_ref, sems, *, sizes
):
    energies, _, order, _ = green_ref.shape
    momentum, core = lax.axis_index("pair"), lax.axis_index("core")
    copies = []
    for e in range(energies):
        for part in range(2):
            source, target = retarded_ref.at[momentum, e, part], green_ref.at[e, part]
            copies.append(pltpu.make_async_copy(source, target, sems.at[e, part]))
            source, target = self_energy_ref.at[0, e, part], sigma_ref.at[e, part]
            copies.append(pltpu.make_async_copy(source, target, sems.at[e, 2 + part]))
    later = (
        pltpu.make_async_copy(energy_ref, energy_out_ref, sems.at[energies, 0]),
        pltpu.make_async_copy(table_ref, table_out_ref, sems.at[energies, 1]),
    )
    for copy in (*copies, *later):
        copy.start()
    greens, crosses = [], []
    per_energy = len(copies) // energies
    for e in range(energies):
        for copy in copies[e * per_energy : (e + 1) * per_energy]:
            copy.wait()
        greens.append(green_ref[e].reshape(2 * order, order))
        by_re, by_im = (dot(greens[e], sigma_ref[e, part]) for part in range(2))
        cross = jnp.concatenate([by_re[:order] - by_im[order:], by_im[:order] + by_re[order:]], axis=0)
        crosses.append(cross.astype(jnp.bfloat16))
    for e in range(energies):
        cross_ref[e] = crosses[e]
    write_blocks(away_ref, greens, crosses, 1 - core, sizes)
    for copy in later:
        copy.wait()


def arrange_kernel(green_ref, cross_ref, energy_ref, table_ref, own_ref, out_ref, pick_ref, *, sizes):
    tile_count, hop_count = sizes
    count = pick_ref.shape[0]
    energies = count // (2 * tile_count * hop_count)
    devices = count // energies
    core = lax.axis_index("core")
    both = range(green_ref.shape[0])
    greens = [green_ref[e].reshape(cross_ref.shape[1:]) for e in both]
    write_blocks(own_ref, greens, [cross_ref[e] for e in both], core, sizes)
    slots = jnp.concatenate([energy_ref[r : r + 1] for r in range(energy_ref.shape[0])], axis=1)
    digit = lax.broadcasted_iota(jnp.int32, (16, count), 0)
    digits = jnp.where(digit == 0, slots >> 1, slots & 1).astype(jnp.float32).astype(jnp.bfloat16)
    column = lax.broadcasted_iota(jnp.int32, (1, count), 1)
    energy = sum((jnp.where(column >= n * devices, 1, 0) for n in range(1, energies)), jnp.zeros_like(column))
    device = column - energy * devices
    side, place = device & 1, device >> 1
    hop = sum((jnp.where(place >= n * tile_count, 1, 0) for n in range(1, hop_count)), jnp.zeros_like(column))
    place = (place - hop * tile_count) * hop_count + hop
    wanted = (place * 2 + side + core - 2 * side * core) * energies + energy
    row = lax.broadcasted_iota(jnp.int32, (count, count), 0)
    taken = dot(digits, one_hot(row == wanted))
    pick_ref[...] = one_hot(row == (2.0 * taken[:1] + taken[1:2]).astype(jnp.int32))
    out_ref[...] = dot(table_ref[: 2 * count], pick_ref[...]).astype(jnp.bfloat16)


def times(left, right):
    return left[0] * right[0] - left[1] * right[1], left[0] * right[1] + left[1] * right[0]


def correlate_kernel(signal_ref, forward_ref, table_ref, out_ref, staged_ref):
    _, count, _ = staged_ref.shape
    devices = signal_ref.shape[0] // 2
    energies = count // devices
    half = signal_ref.shape[1] // (2 * energies)
    gap = jnp.zeros((devices, LANES - half), staged_ref.dtype)
    for component in range(2):
        signal = signal_ref[component * devices : (component + 1) * devices]
        for e in range(energies):
            for part in range(2):
                staged_ref[component, e * devices : (e + 1) * devices, part * LANES : (part + 1) * LANES] = jnp.concatenate(
                    [piece(signal, 2 * e + part), gap], axis=1
                )
    spectra = []
    for component in range(2):
        cos_sum, sin_sum = (dot(forward_ref[r * count : (r + 1) * count], staged_ref[component]) for r in range(2))
        turned = (sin_sum[:, LANES:], -sin_sum[:, :LANES])
        plain = (cos_sum[:, :LANES], cos_sum[:, LANES:])
        spectra.append([[p + t for p, t in zip(plain, turned)], [p - t for p, t in zip(plain, turned)]])
    one, two = spectra
    ahead, behind = times(one[0], two[1]), times(one[1], two[0])
    even_parts = [ahead[0] + behind[0], ahead[1] + behind[1]]
    odd_parts = [behind[1] - ahead[1], ahead[0] - behind[0]]
    even_parts = jnp.concatenate(even_parts, axis=1).astype(jnp.bfloat16)
    odd_parts = jnp.concatenate(odd_parts, axis=1).astype(jnp.bfloat16)
    size = count // CHUNKS
    rows = size // 2
    for n in range(CHUNKS):
        even = dot(table_ref[2 * count + n * size : 2 * count + (n + 1) * size], even_parts)
        odd = dot(table_ref[3 * count + n * size : 3 * count + (n + 1) * size], odd_parts)
        for component, total in enumerate((even + odd, even - odd)):
            total = total.astype(out_ref.dtype)
            im, re = total[:, LANES : LANES + half], total[:, :half]
            out_ref[component, n * rows : (n + 1) * rows] = packed([im[:rows], re[:rows], im[rows:], re[rows:]])


def place_kernel(gathered_ref, out_ref, placed_ref, sems, *, scale):
    _, lags, _, tiles, order = out_ref.shape
    half, low = order // 2, lags // 2
    rows = low * tiles
    target = lax.broadcasted_iota(jnp.int32, (rows, rows), 0)
    source = lax.broadcasted_iota(jnp.int32, (rows, rows), 1)
    pick = one_hot((source & (low - 1)) * tiles + (source >> (low.bit_length() - 1)) == target)
    copies = []
    for high in range(2):
        for part in range(2):
            both = [piece(gathered_ref[side * rows : (side + 1) * rows], 2 * high + part) for side in range(2)]
            moved = dot(pick, jnp.concatenate(both, axis=1)) * (-scale if part else scale)
            for lag in range(low):
                placed_ref[high, part, lag] = moved[lag * tiles : (lag + 1) * tiles]
            copies.append(
                pltpu.make_async_copy(
                    placed_ref.at[high, part], out_ref.at[0, pl.ds(high * low, low), part], sems.at[high, part]
                )
            )
            copies[-1].start()
    for copy in copies:
        copy.wait()


def on_chip(array):
    return pltpu.with_memory_space_constraint(array, pltpu.VMEM) if not INTERPRET else array


def off_chip(array):
    return pltpu.with_memory_space_constraint(array, pltpu.HBM) if not INTERPRET else array


def on_chip_out(shape, dtype):
    return pltpu.VMEM(shape, dtype) if not INTERPRET else jax.ShapeDtypeStruct(shape, dtype)


def body(retarded, self_energy, energy_of, *, sizes):
    tile_count, hop_count = sizes
    energies, order = retarded.shape[1], retarded.shape[3]
    half = order // 2
    slot_count = energy_of.shape[0]
    in_vmem = pl.BlockSpec(memory_space=pltpu.VMEM)
    in_place = pl.BlockSpec(memory_space=pl.ANY)
    cos_part, sin_part = twiddles(slot_count)
    lag_count = slot_count // tile_count
    lags = np.arange(slot_count).reshape(tile_count, 2, lag_count // 2).transpose(1, 0, 2).reshape(-1)
    lags = lags.reshape(2, CHUNKS, -1).transpose(1, 0, 2).reshape(-1)
    table = jnp.asarray(np.concatenate([cos_part, sin_part, cos_part.T[lags], sin_part.T[lags]]), jnp.bfloat16)
    lanes = math.gcd(slot_count, LANES)
    slot_energy = energy_of.reshape(slot_count // lanes, lanes)
    block = on_chip_out((order, 2 * energies * half), jnp.bfloat16)
    greens = on_chip_out((energies, 2, order, order), jnp.bfloat16)
    crosses = on_chip_out((energies, 2 * order, order), jnp.bfloat16)
    away, green, cross, slot_energy, table = pl.pallas_call(
        functools.partial(triple_kernel, sizes=sizes),
        out_shape=(
            block,
            greens,
            crosses,
            on_chip_out(slot_energy.shape, jnp.int32),
            on_chip_out(table.shape, jnp.bfloat16),
        ),
        in_specs=[in_place] * 4,
        out_specs=(in_vmem,) * 5,
        scratch_shapes=[
            pltpu.VMEM((energies, 2, order, order), jnp.bfloat16),
            pltpu.SemaphoreType.DMA((energies + 1, 4)),
        ],
        compiler_params=SCHEDULE,
        interpret=INTERPRET,
        name="triple",
    )(*(off_chip(array) for array in (retarded, self_energy, slot_energy, table)))
    sibling = lax.ppermute(away, "core", [(0, 1), (1, 0)])
    own, forward = pl.pallas_call(
        functools.partial(arrange_kernel, sizes=sizes),
        out_shape=(block, on_chip_out((2 * slot_count, slot_count), jnp.bfloat16)),
        in_specs=[in_vmem] * 4,
        out_specs=(in_vmem,) * 2,
        scratch_shapes=[pltpu.VMEM((slot_count, slot_count), jnp.bfloat16)],
        compiler_params=SCHEDULE,
        interpret=INTERPRET,
        name="arrange",
    )(on_chip(green), on_chip(cross), on_chip(slot_energy), on_chip(table))
    blocks, forward = lax.optimization_barrier((jnp.stack([own, sibling], axis=1), forward))
    gathered = lax.all_to_all(blocks, ("mem", "zh", "tile"), split_axis=0, concat_axis=0, tiled=True)
    polar = pl.pallas_call(
        correlate_kernel,
        out_shape=on_chip_out((2, slot_count // 2, 4 * half), jnp.bfloat16),
        in_specs=[in_vmem] * 3,
        out_specs=in_vmem,
        scratch_shapes=[pltpu.VMEM((2, slot_count, 2 * LANES), jnp.bfloat16)],
        compiler_params=SCHEDULE,
        interpret=INTERPRET,
        name="correlate",
    )(on_chip(gathered.reshape(2 * order, 2 * energies * half)), on_chip(forward), on_chip(table))
    packed = polar.reshape(2 * tile_count, lag_count // 2, 4 * half)
    regrouped = lax.all_to_all(packed, ("mem", "tile"), split_axis=0, concat_axis=0, tiled=True)
    return pl.pallas_call(
        functools.partial(place_kernel, scale=1.0 / (2 * slot_count * math.sqrt(slot_count))),
        out_shape=jax.ShapeDtypeStruct((1, lag_count, 2, tile_count, order), jnp.float32),
        in_specs=[in_vmem],
        out_specs=in_place,
        scratch_shapes=[
            pltpu.VMEM((2, 2, lag_count // 2, tile_count, order), jnp.float32),
            pltpu.SemaphoreType.DMA((2, 2)),
        ],
        compiler_params=SCHEDULE,
        interpret=INTERPRET,
        name="place",
    )(on_chip(regrouped.reshape(tile_count * lag_count, 4 * half)))


def solution(mesh):
    comp, tile, rep = mesh.devices.shape
    split = Mesh(mesh.devices.reshape(2, comp // 2, tile, rep // 2, 2), ("pair", "mem", "tile", "zh", "core"))
    energy_axes = ("tile", "zh", "core")
    placed = (
        P(None, energy_axes, None, None, None),
        P(("pair", "mem"), energy_axes, None, None, None),
        P(),
    )
    return jax.shard_map(
        functools.partial(body, sizes=(tile, rep // 2)),
        mesh=split,
        in_specs=placed,
        out_specs=P(("pair", "mem"), "tile", None, ("zh", "core"), None),
        check_vma=False,
    )
```
